32 devices in a mesh: row: 8 (over z, x), col: 4 (over y, core).
Axes of the slice: x: 2, y: 2, z: 4, core: 2. Of those that a mesh axis runs over, the one named last changes fastest.
Arguments:
- krylov_block: bfloat16 [64, 16384], P(None, ('row', 'col')), may hold values from -54 to 54
- degree: int32 [16384], P(('row', 'col')), may hold values from 16 to 64
- tile_values: bfloat16 [256, 4, 64, 512], P('row', 'col'), may hold values from -6 to 6
- tile_column: int32 [256, 4, 8], P('row', 'col'), may hold values from 0 to 63
- tile_live: int32 [256, 4, 8], P('row', 'col'), may hold values 0 or 1
Outputs:
- orthonormal: float32 [64, 16384], P(None, ('row', 'col'))
- quotient: float32 [64, 64], replicated
The draws below stay inside these ranges and needn't reach their ends.
All inputs are finite; a program needn't handle non-finite values. No bound on the sum of `tile_live` on one device may be relied on, other than what follows from the above.
Results may differ from the reference program's by a relative error of at most 0.0032.
Values may be sent and summed in bfloat16 or wider, within the bound.
No kernel may reach another device: no remote copies, remote signals or barrier semaphores. Data moves between devices by JAX's collectives and lax.ppermute only.
A program may use at most 128 MiB of HBM per device.

```python
import math
import jax
import jax.numpy as jnp
from jax import lax

VECTORS = 64
TILE = 64
SLOTS = 8
VERTS_DEV = 512
SOURCES = 8
GROUPS = 4
VERTICES = 16384
ALL_BLOCKS = 256


def draw_krylov_block(key, part):
    subkeys = jax.random.split(key, 3)
    position = jnp.arange(VERTICES, dtype=jnp.float32) / VERTICES
    rising = 0.5 + position
    column_scale = jnp.exp(jax.random.uniform(subkeys[0], (VECTORS, 1), minval=math.log(0.3), maxval=math.log(3.0)))
    row_scale = jnp.exp(jax.random.uniform(subkeys[1], (VERTICES,), minval=math.log(0.3), maxval=math.log(3.0)))
    values = jnp.clip(jax.random.normal(subkeys[2], (VECTORS, VERTICES)), -4.0, 4.0)
    return (values * column_scale * (row_scale * rising)[None, :]).astype(jnp.bfloat16)


def touch_ends(drawn, own_key, low, largest):
    place = [jax.random.randint(jax.random.fold_in(own_key, axis), (), 0, length) for axis, length in enumerate(drawn.shape)]
    widest = drawn.shape.index(max(drawn.shape))
    next_to = place[:widest] + [(place[widest] + 1) % drawn.shape[widest]] + place[widest + 1:]
    return drawn.at[tuple(place)].set(low).at[tuple(next_to)].set(largest)


def levels(own_key, shape, shards, least, top_value):
    factor_of, own = 1.0, jax.random.fold_in(own_key, 6)
    for axis_at, parts in shards:
        heights = jnp.exp(jax.random.uniform(jax.random.fold_in(own, axis_at), (parts,), jnp.float32, least / len(shards), top_value / len(shards)))
        factor_of = factor_of * jnp.repeat(heights, shape[axis_at] // parts).reshape([-1 if axis == axis_at else 1 for axis in range(len(shape))])
    return factor_of


def bell_draw(rng, dims, scale, reach, pieces=(), held_as=jnp.bfloat16):
    loudness = levels(rng, dims, pieces, -0.22, 0.18) if pieces else 1.0
    drawn = jax.random.normal(rng, dims, jnp.float32) * scale * loudness
    return jnp.minimum(jnp.maximum(drawn, -reach), reach).astype(held_as)


def setup_inputs(seed: int = 0) -> dict:
    streams_of = jax.random.split(jax.random.key(seed), 6)
    krylov_block = draw_krylov_block(jax.random.fold_in(streams_of[5], 71), 0)
    degree = touch_ends(jax.random.randint(streams_of[1], (VERTICES,), 16, 65), jax.random.fold_in(streams_of[1], 1), 16, 64).astype(jnp.int32)
    tile_values = bell_draw(streams_of[2], (ALL_BLOCKS, GROUPS, TILE, SLOTS * TILE), 1.0, 6.0, ((0, 8), (1, 4)))
    tile_column = touch_ends(jax.random.randint(streams_of[3], (ALL_BLOCKS, GROUPS, SLOTS), 0, SOURCES * VERTS_DEV // TILE), jax.random.fold_in(streams_of[3], 1), 0, (SOURCES * VERTS_DEV // TILE) - 1).astype(jnp.int32)
    tile_live = touch_ends((jax.random.randint(streams_of[4], (ALL_BLOCKS, GROUPS, SLOTS), 0, 4) < 3).astype(jnp.int32), jax.random.fold_in(streams_of[4], 1), 0, 1)
    return dict(krylov_block=krylov_block, degree=degree, tile_values=tile_values, tile_column=tile_column, tile_live=tile_live)


def gram_of(left, right):
    return lax.dot_general(left.astype(jnp.float32), right.astype(jnp.float32), (((1,), (1,)), ((), ())), precision=lax.Precision.HIGHEST, preferred_element_type=jnp.float32)

def reference(krylov_block, degree, tile_values, tile_column, tile_live):
    inv_root = lax.rsqrt(degree.astype(jnp.float32))
    basis_wide = krylov_block.astype(jnp.float32)
    scaled = (basis_wide * inv_root[None, :]).astype(jnp.bfloat16)
    blocks = scaled.reshape(VECTORS, VERTICES // TILE, TILE)
    per_piece = VERTS_DEV // TILE

    def add_group(group, running):
        group = jnp.asarray(group).astype(jnp.int32)
        panel = lax.dynamic_index_in_dim(tile_values, group, 1, keepdims=False).astype(jnp.float32)
        column = lax.dynamic_index_in_dim(tile_column, group, 1, keepdims=False)
        live_part = lax.dynamic_index_in_dim(tile_live, group, 1, keepdims=False)
        source = column // per_piece
        within = column % per_piece
        pick_index = ((source * GROUPS + group) * per_piece + within).astype(jnp.int32)
        chosen = jnp.take(blocks, pick_index.reshape(-1), axis=1).astype(jnp.float32)
        chosen = chosen * live_part.reshape(1, -1, 1).astype(jnp.float32)
        chosen = chosen.reshape(VECTORS, ALL_BLOCKS, SLOTS * TILE)
        product = jnp.einsum('klc,luc->klu', chosen, panel, precision=lax.Precision.HIGHEST)
        return running + product.reshape(VECTORS, VERTICES)
    spread = lax.fori_loop(0, GROUPS, add_group, jnp.zeros((VECTORS, VERTICES), jnp.float32))
    applied = basis_wide - inv_root[None, :] * spread
    quotient = gram_of(basis_wide, applied) / VERTICES
    energy = gram_of(applied, applied)
    factor = jnp.linalg.cholesky(energy)
    identity = jnp.eye(VECTORS, dtype=jnp.float32)
    inverse = lax.linalg.triangular_solve(factor, identity, left_side=True, lower=True)
    orthonormal = jnp.dot(inverse, applied, precision=lax.Precision.HIGHEST) * math.sqrt(VERTICES)
    return (orthonormal, quotient)
```

```python
import math

import jax
import jax.numpy as jnp
from jax import lax
from jax.experimental import pallas as pl
from jax.experimental.pallas import tpu as pltpu
from jax.sharding import PartitionSpec as P

F32 = jnp.float32
BF16 = jnp.bfloat16


def vmem():
    return pl.BlockSpec(memory_space=pltpu.VMEM)


def smem():
    return pl.BlockSpec(memory_space=pltpu.SMEM)


def swap(value, axis, size, mask):
    return lax.ppermute(value, axis, [(i, i ^ mask) for i in range(size)])


def bits(size):
    out = []
    mask = 1
    while mask < size:
        out.append(mask)
        mask *= 2
    return out


def split3(value):
    high = value.astype(BF16)
    rest = value - high.astype(F32)
    mid = rest.astype(BF16)
    low = (rest - mid.astype(F32)).astype(BF16)
    return high, mid, low


def scale_kernel(basis_ref, degree_ref, left_ref, right_ref):
    half = left_ref.shape[1]
    inv_root = lax.rsqrt(degree_ref[...].astype(F32))
    scaled = (basis_ref[...].astype(F32) * inv_root).astype(BF16)
    left_ref[...] = scaled[:, :half]
    right_ref[...] = scaled[:, half:]


def tile_kernel(sources, groups, per_piece, left_order, right_order, column_ref, live_ref, left_ref, right_ref,
                panel_ref, keep_ref, send_ref, table_ref, lhs_ref):
    vectors = left_ref.shape[1]
    half = left_ref.shape[2]
    height = panel_ref.shape[1]
    slots = column_ref.shape[1]
    wide = 2 * height
    pairs = half // wide
    my_row = lax.axis_index("row")
    my_col = lax.axis_index("col")
    zero_at = sources * per_piece
    for side, order, ref in ((0, left_order, left_ref), (1, right_order, right_ref)):
        for at in range(sources):
            for pair in range(pairs):
                tile = ref[at, :, pair * wide:(pair + 1) * wide]
                block = order[at] * per_piece + 2 * (side * pairs + pair)
                table_ref[block] = tile
                table_ref[block + 1] = jnp.concatenate([tile[:, height:], tile[:, :height]], axis=1)
    table_ref[zero_at] = jnp.zeros((vectors, wide), BF16)
    lane = lax.broadcasted_iota(jnp.int32, (vectors, wide), 1)
    is_low = lane < height
    turn = my_row * per_piece
    pack = 4
    chunks = per_piece // pack

    def group(piece_at, chunk, slot_of):
        row0 = (piece_at ^ my_col) * per_piece + chunk * pack
        for inner in range(pack):
            row = row0 + inner
            for pair in range(slots // 2):
                first = column_ref[row, 2 * pair] ^ turn
                second = column_ref[row, 2 * pair + 1] ^ turn ^ 1
                first = jnp.where(live_ref[row, 2 * pair] == 1, first, zero_at)
                second = jnp.where(live_ref[row, 2 * pair + 1] == 1, second, zero_at)
                lhs_ref[slot_of, inner * vectors:(inner + 1) * vectors, pair * wide:(pair + 1) * wide] = jnp.where(
                    is_low, table_ref[first], table_ref[second])
        rhs = panel_ref[pl.ds(row0, pack)].reshape(pack * height, slots * height)
        prod = lax.dot_general(lhs_ref[slot_of], rhs, (((1,), (1,)), ((), ())), preferred_element_type=F32)
        out = []
        for pair in range(pack // 2):
            lanes = slice(pair * wide, (pair + 1) * wide)
            top = prod[2 * pair * vectors:(2 * pair + 1) * vectors, lanes]
            low = prod[(2 * pair + 1) * vectors:(2 * pair + 2) * vectors, lanes]
            out.append(jnp.where(is_low, top, low))
        return jnp.concatenate(out, axis=1)

    span = pack * height
    if groups <= 4:
        at = 0
        for piece in [s for s in range(groups) if s % 2] + [s for s in range(groups) if s % 2 == 0]:
            for chunk in range(chunks):
                value = group(piece, chunk, at % 2)
                at += 1
                lanes = slice(chunk * span, (chunk + 1) * span)
                if piece % 2:
                    send_ref[piece // 2, :, lanes] = value.astype(BF16)
                else:
                    keep_ref[piece // 2, :, lanes] = value
    else:
        def body(step, carry):
            for chunk in range(chunks):
                lanes = slice(chunk * span, (chunk + 1) * span)
                send_ref[step, :, lanes] = group(2 * step + 1, chunk, 0).astype(BF16)
                keep_ref[step, :, lanes] = group(2 * step, chunk, 1)
            return carry

        lax.fori_loop(0, groups // 2, body, 0)


def gram_kernel(received, basis_ref, degree_ref, keep_ref, *refs):
    parts = refs[:received]
    split_ref, gram_ref, stack_ref = refs[received:]
    vectors = basis_ref.shape[0]
    spread = keep_ref[0]
    for ref in parts:
        spread = spread + ref[0].astype(F32)
    basis = basis_ref[...]
    inv_root = lax.rsqrt(degree_ref[...].astype(F32))
    applied = basis.astype(F32) - inv_root * spread
    for at, piece in enumerate(split3(applied)):
        split_ref[at * vectors:(at + 1) * vectors, :] = piece
        stack_ref[at * vectors:(at + 1) * vectors, :] = piece
    stack_ref[3 * vectors:4 * vectors, :] = basis
    stack = stack_ref[...]
    prod = lax.dot_general(stack, stack, (((1,), (1,)), ((), ())), preferred_element_type=F32)
    wide = 2 * vectors
    near = prod[:, :wide]
    far = prod[:, wide:]

    def rows(value, at):
        return value[at * vectors:(at + 1) * vectors]

    energy_low = rows(near, 0) + (rows(near, 1) + (rows(near, 2) + rows(far, 0)))
    energy_high = rows(near, 0) + rows(near, 1)
    quotient_low = rows(near, 3) + rows(far, 3)
    quotient_high = rows(near, 3)
    lane = lax.broadcasted_iota(jnp.int32, (vectors, wide), 1)
    gram_ref[...] = jnp.where(
        lane < vectors,
        energy_low + pltpu.roll(energy_high, vectors, 1),
        quotient_high + pltpu.roll(quotient_low, vectors, 1),
    )


def finish_kernel(total_rows, gram_ref, split_ref, out_ref, quotient_ref):
    vectors = gram_ref.shape[0]
    wide = 2 * vectors
    gram = gram_ref[...]
    quotient_ref[...] = (gram / total_rows)[:, vectors:]
    row = lax.broadcasted_iota(jnp.int32, (vectors, wide), 0)
    lane = lax.broadcasted_iota(jnp.int32, (vectors, wide), 1)
    work = jnp.where(lane < vectors, gram, jnp.where(lane == row + vectors, 1.0, 0.0))
    height = 8
    tiles = [work[at * height:(at + 1) * height] for at in range(vectors // height)]
    row8 = lax.broadcasted_iota(jnp.int32, (height, wide), 0)
    for step in range(vectors):
        home = step // height
        own = tiles[home][step % height:step % height + 1]
        scaled = own / own[:, step:step + 1]
        for at in range(home, vectors // height):
            column = tiles[at][:, step:step + 1]
            change = column * scaled
            if at == home:
                change = jnp.where(row8 > step % height, change, 0.0)
            tiles[at] = tiles[at] - change
    done = jnp.concatenate(tiles, axis=0)
    pivot = jnp.sum(jnp.where(lane == row, done, 0.0), axis=1, keepdims=True)
    inverse = done * (lax.rsqrt(pivot) * math.sqrt(total_rows))
    inverse = inverse[:, vectors:]
    w_high, w_mid, w_low = split3(inverse)
    left = jnp.concatenate([w_high, w_high, w_high, w_mid, w_mid, w_low], axis=1)
    pieces = split_ref[...]
    right = jnp.concatenate([pieces, pieces[:2 * vectors], pieces[:vectors]], axis=0)
    out_ref[...] = jnp.dot(left, right, preferred_element_type=F32)


def on_device(krylov_block, degree, tile_values, tile_column, tile_live):
    vectors, owned = krylov_block.shape
    block_rows, _, height, slot_width = tile_values.shape
    sources = lax.axis_size("row")
    groups = lax.axis_size("col")
    per_piece = owned // height
    half = owned // 2
    degree_row = degree.reshape(1, owned)
    left, right = pl.pallas_call(
        scale_kernel,
        out_shape=[jax.ShapeDtypeStruct((vectors, half), BF16)] * 2,
        in_specs=[vmem(), vmem()],
        out_specs=[vmem(), vmem()],
        name="scale",
    )(krylov_block, degree_row)
    row_bits = bits(sources)
    left_bits = row_bits[:0:-1] + row_bits[:1]
    right_bits = row_bits[:1] + row_bits[:0:-1]
    left, right = left[None], right[None]
    left_order, right_order = [0], [0]
    for left_bit, right_bit in zip(left_bits, right_bits):
        new_left = swap(left, "row", sources, left_bit)
        new_right = swap(right, "row", sources, right_bit)
        left = jnp.concatenate([left, new_left], axis=0)
        right = jnp.concatenate([right, new_right], axis=0)
        left_order = left_order + [at ^ left_bit for at in left_order]
        right_order = right_order + [at ^ right_bit for at in right_order]
    many = groups // 2
    keep, send = pl.pallas_call(
        lambda *refs: tile_kernel(sources, groups, per_piece, left_order, right_order, *refs),
        out_shape=[
            jax.ShapeDtypeStruct((many, vectors, owned), F32),
            jax.ShapeDtypeStruct((many, vectors, owned), BF16),
        ],
        in_specs=[smem(), smem(), vmem(), vmem(), vmem()],
        out_specs=[vmem(), vmem()],
        scratch_shapes=[
            pltpu.VMEM((sources * per_piece + 1, vectors, 2 * height), BF16),
            pltpu.VMEM((2, 4 * vectors, slot_width), BF16),
        ],
        compiler_params=pltpu.CompilerParams(vmem_limit_bytes=48 << 20),
        name="tiles",
    )(tile_column[:, 0], tile_live[:, 0], left, right, tile_values[:, 0])
    running = keep
    received = []
    for bit in bits(groups):
        got = swap(send, "col", groups, bit)
        received.append(got)
        if running.shape[0] > 1:
            summed = running + got.astype(F32)
            pairs = summed.reshape((-1, 2) + summed.shape[1:])
            running, send = pairs[:, 0], pairs[:, 1].astype(BF16)
    pieces, gram = pl.pallas_call(
        lambda *refs: gram_kernel(len(received), *refs),
        out_shape=[
            jax.ShapeDtypeStruct((3 * vectors, owned), BF16),
            jax.ShapeDtypeStruct((vectors, 2 * vectors), F32),
        ],
        in_specs=[vmem()] * (3 + len(received)),
        out_specs=[vmem(), vmem()],
        scratch_shapes=[pltpu.VMEM((4 * vectors, owned), BF16)],
        name="gram",
    )(krylov_block, degree_row, keep, *received)
    for axis, size in (("col", groups), ("row", sources)):
        for bit in bits(size):
            gram = gram + swap(gram, axis, size, bit)
    total_rows = sources * groups * owned
    orthonormal, quotient = pl.pallas_call(
        lambda *refs: finish_kernel(total_rows, *refs),
        out_shape=[
            jax.ShapeDtypeStruct((vectors, owned), F32),
            jax.ShapeDtypeStruct((vectors, vectors), F32),
        ],
        in_specs=[vmem(), vmem()],
        out_specs=[vmem(), vmem()],
        name="finish",
    )(gram, pieces)
    return (orthonormal, quotient)


def solution(mesh):
    return jax.shard_map(
        on_device,
        mesh=mesh,
        in_specs=(
            P(None, ("row", "col")),
            P(("row", "col")),
            P("row", "col", None, None),
            P("row", "col", None),
            P("row", "col", None),
        ),
        out_specs=(P(None, ("row", "col")), P()),
        check_vma=False,
    )
```

```python
import math

import jax
import jax.numpy as jnp
from jax import lax
from jax.experimental import pallas as pl
from jax.experimental.pallas import tpu as pltpu
from jax.sharding import PartitionSpec as P

F32 = jnp.float32
BF16 = jnp.bfloat16


def limit(mib):
    return pltpu.CompilerParams(vmem_limit_bytes=mib << 20)


def vmem():
    return pl.BlockSpec(memory_space=pltpu.VMEM)


def smem():
    return pl.BlockSpec(memory_space=pltpu.SMEM)


def swap(value, axis, size, mask):
    return lax.ppermute(value, axis, [(i, i ^ mask) for i in range(size)])


def bits(size):
    out = []
    mask = 1
    while mask < size:
        out.append(mask)
        mask *= 2
    return out


def split3(value):
    high = value.astype(BF16)
    rest = value - high.astype(F32)
    mid = rest.astype(BF16)
    low = (rest - mid.astype(F32)).astype(BF16)
    return high, mid, low


def scale_kernel(basis_ref, degree_ref, left_ref, right_ref):
    half = left_ref.shape[1]
    inv_root = lax.rsqrt(degree_ref[...].astype(F32))
    scaled = (basis_ref[...].astype(F32) * inv_root).astype(BF16)
    left_ref[...] = scaled[:, :half]
    right_ref[...] = scaled[:, half:]


def tile_kernel(sources, groups, per_piece, left_order, right_order, column_ref, live_ref, left_ref, right_ref,
                panel_ref, keep_ref, send_ref, table_ref, lhs_ref):
    vectors = left_ref.shape[1]
    half = left_ref.shape[2]
    height = panel_ref.shape[1]
    slots = column_ref.shape[0]
    wide = 2 * height
    pairs = half // wide
    my_row = lax.axis_index("row")
    my_col = lax.axis_index("col")
    zero_at = sources * per_piece
    for side, order, ref in ((0, left_order, left_ref), (1, right_order, right_ref)):
        for at in range(sources):
            for pair in range(pairs):
                tile = ref[at, :, pair * wide:(pair + 1) * wide]
                block = order[at] * per_piece + 2 * (side * pairs + pair)
                table_ref[block] = tile
                table_ref[block + 1] = jnp.concatenate([tile[:, height:], tile[:, :height]], axis=1)
    table_ref[zero_at] = jnp.zeros((vectors, wide), BF16)
    lane = lax.broadcasted_iota(jnp.int32, (vectors, wide), 1)
    is_low = lane < height
    turn = my_row * per_piece
    pack = 4
    chunks = per_piece // pack

    def group(piece_at, chunk, slot_of):
        row0 = (piece_at ^ my_col) * per_piece + chunk * pack
        for inner in range(pack):
            row = row0 + inner
            for pair in range(slots // 2):
                first = column_ref[2 * pair, row] ^ turn
                second = column_ref[2 * pair + 1, row] ^ turn ^ 1
                first = jnp.where(live_ref[2 * pair, row] == 1, first, zero_at)
                second = jnp.where(live_ref[2 * pair + 1, row] == 1, second, zero_at)
                lhs_ref[slot_of, inner * vectors:(inner + 1) * vectors, pair * wide:(pair + 1) * wide] = jnp.where(
                    is_low, table_ref[first], table_ref[second])
        rhs = panel_ref[pl.ds(row0, pack)].reshape(pack * height, slots * height)
        prod = lax.dot_general(lhs_ref[slot_of], rhs, (((1,), (1,)), ((), ())), preferred_element_type=F32)
        out = []
        for pair in range(pack // 2):
            lanes = slice(pair * wide, (pair + 1) * wide)
            top = prod[2 * pair * vectors:(2 * pair + 1) * vectors, lanes]
            low = prod[(2 * pair + 1) * vectors:(2 * pair + 2) * vectors, lanes]
            out.append(jnp.where(is_low, top, low))
        return jnp.concatenate(out, axis=1)

    span = pack * height
    if groups <= 4:
        at = 0
        for piece in [s for s in range(groups) if s % 2] + [s for s in range(groups) if s % 2 == 0]:
            for chunk in range(chunks):
                value = group(piece, chunk, at % 2)
                at += 1
                lanes = slice(chunk * span, (chunk + 1) * span)
                if piece % 2:
                    send_ref[piece // 2, :, lanes] = value.astype(BF16)
                else:
                    keep_ref[piece // 2, :, lanes] = value
    else:
        def body(step, carry):
            for chunk in range(chunks):
                lanes = slice(chunk * span, (chunk + 1) * span)
                send_ref[step, :, lanes] = group(2 * step + 1, chunk, 0).astype(BF16)
                keep_ref[step, :, lanes] = group(2 * step, chunk, 1)
            return carry

        lax.fori_loop(0, groups // 2, body, 0)


def gram_kernel(received, basis_ref, degree_ref, keep_ref, *refs):
    parts = refs[:received]
    split_ref, gram_ref, stack_ref = refs[received:]
    vectors = basis_ref.shape[0]
    spread = keep_ref[0]
    for ref in parts:
        spread = spread + ref[0].astype(F32)
    basis = basis_ref[...]
    inv_root = lax.rsqrt(degree_ref[...].astype(F32))
    applied = basis.astype(F32) - inv_root * spread
    for at, piece in enumerate(split3(applied)):
        split_ref[at * vectors:(at + 1) * vectors, :] = piece
        stack_ref[at * vectors:(at + 1) * vectors, :] = piece
    stack_ref[3 * vectors:4 * vectors, :] = basis
    stack = stack_ref[...]
    prod = lax.dot_general(stack, stack, (((1,), (1,)), ((), ())), preferred_element_type=F32)
    wide = 2 * vectors
    near = prod[:, :wide]
    far = prod[:, wide:]

    def rows(value, at):
        return value[at * vectors:(at + 1) * vectors]

    energy_low = rows(near, 0) + (rows(near, 1) + (rows(near, 2) + rows(far, 0)))
    energy_high = rows(near, 0) + rows(near, 1)
    quotient_low = rows(near, 3) + rows(far, 3)
    quotient_high = rows(near, 3)
    lane = lax.broadcasted_iota(jnp.int32, (vectors, wide), 1)
    gram_ref[...] = jnp.where(
        lane < vectors,
        energy_low + pltpu.roll(energy_high, vectors, 1),
        quotient_high + pltpu.roll(quotient_low, vectors, 1),
    )


def finish_kernel(total_rows, gram_ref, split_ref, out_ref, quotient_ref):
    vectors = gram_ref.shape[0]
    wide = 2 * vectors
    gram = gram_ref[...]
    quotient_ref[...] = (gram / total_rows)[:, vectors:]
    row = lax.broadcasted_iota(jnp.int32, (vectors, wide), 0)
    lane = lax.broadcasted_iota(jnp.int32, (vectors, wide), 1)
    work = jnp.where(lane < vectors, gram, jnp.where(lane == row + vectors, 1.0, 0.0))
    height = 8
    tiles = [work[at * height:(at + 1) * height] for at in range(vectors // height)]
    row8 = lax.broadcasted_iota(jnp.int32, (height, wide), 0)
    for step in range(vectors):
        home = step // height
        own = tiles[home][step % height:step % height + 1]
        scaled = own / own[:, step:step + 1]
        for at in range(home, vectors // height):
            column = tiles[at][:, step:step + 1]
            change = column * scaled
            if at == home:
                change = jnp.where(row8 > step % height, change, 0.0)
            tiles[at] = tiles[at] - change
    done = jnp.concatenate(tiles, axis=0)
    pivot = jnp.sum(jnp.where(lane == row, done, 0.0), axis=1, keepdims=True)
    inverse = done * (lax.rsqrt(pivot) * math.sqrt(total_rows))
    inverse = inverse[:, vectors:]
    w_high, w_mid, w_low = split3(inverse)
    left = jnp.concatenate([w_high, w_high, w_high, w_mid, w_mid, w_low], axis=1)
    pieces = split_ref[...]
    right = jnp.concatenate([pieces, pieces[:2 * vectors], pieces[:vectors]], axis=0)
    out_ref[...] = jnp.dot(left, right, preferred_element_type=F32)


def on_device(krylov_block, degree, tile_values, tile_column, tile_live):
    vectors, owned = krylov_block.shape
    block_rows, _, height, slot_width = tile_values.shape
    sources = lax.axis_size("row")
    groups = lax.axis_size("col")
    per_piece = owned // height
    half = owned // 2
    degree_row = degree.reshape(1, owned)
    left, right = pl.pallas_call(
        scale_kernel,
        out_shape=[jax.ShapeDtypeStruct((vectors, half), BF16)] * 2,
        in_specs=[vmem(), vmem()],
        out_specs=[vmem(), vmem()],
        compiler_params=limit(2),
        name="scale",
    )(krylov_block, degree_row)
    row_bits = bits(sources)
    left_bits = row_bits[:0:-1] + row_bits[:1]
    right_bits = row_bits[:1] + row_bits[:0:-1]
    left, right = left[None], right[None]
    left_order, right_order = [0], [0]
    for left_bit, right_bit in zip(left_bits, right_bits):
        new_left = swap(left, "row", sources, left_bit)
        new_right = swap(right, "row", sources, right_bit)
        left = jnp.concatenate([left, new_left], axis=0)
        right = jnp.concatenate([right, new_right], axis=0)
        left_order = left_order + [at ^ left_bit for at in left_order]
        right_order = right_order + [at ^ right_bit for at in right_order]
    many = groups // 2
    keep, send = pl.pallas_call(
        lambda *refs: tile_kernel(sources, groups, per_piece, left_order, right_order, *refs),
        out_shape=[
            jax.ShapeDtypeStruct((many, vectors, owned), F32),
            jax.ShapeDtypeStruct((many, vectors, owned), BF16),
        ],
        in_specs=[smem(), smem(), vmem(), vmem(), vmem()],
        out_specs=[vmem(), vmem()],
        scratch_shapes=[
            pltpu.VMEM((sources * per_piece + 1, vectors, 2 * height), BF16),
            pltpu.VMEM((2, 4 * vectors, slot_width), BF16),
        ],
        compiler_params=limit(12),
        name="tiles",
    )(tile_column[:, 0].T, tile_live[:, 0].T, left, right, tile_values[:, 0])
    running = keep
    received = []
    for bit in bits(groups):
        got = swap(send, "col", groups, bit)
        received.append(got)
        if running.shape[0] > 1:
            summed = running + got.astype(F32)
            pairs = summed.reshape((-1, 2) + summed.shape[1:])
            running, send = pairs[:, 0], pairs[:, 1].astype(BF16)
    pieces, gram = pl.pallas_call(
        lambda *refs: gram_kernel(len(received), *refs),
        out_shape=[
            jax.ShapeDtypeStruct((3 * vectors, owned), BF16),
            jax.ShapeDtypeStruct((vectors, 2 * vectors), F32),
        ],
        in_specs=[vmem()] * (3 + len(received)),
        out_specs=[vmem(), vmem()],
        scratch_shapes=[pltpu.VMEM((4 * vectors, owned), BF16)],
        compiler_params=limit(4),
        name="gram",
    )(krylov_block, degree_row, keep, *received)
    for axis, size in (("col", groups), ("row", sources)):
        for bit in bits(size):
            gram = gram + swap(gram, axis, size, bit)
    total_rows = sources * groups * owned
    orthonormal, quotient = pl.pallas_call(
        lambda *refs: finish_kernel(total_rows, *refs),
        out_shape=[
            jax.ShapeDtypeStruct((vectors, owned), F32),
            jax.ShapeDtypeStruct((vectors, vectors), F32),
        ],
        in_specs=[vmem(), vmem()],
        out_specs=[vmem(), vmem()],
        compiler_params=limit(4),
        name="finish",
    )(gram, pieces)
    return (orthonormal, quotient)


def solution(mesh):
    return jax.shard_map(
        on_device,
        mesh=mesh,
        in_specs=(
            P(None, ("row", "col")),
            P(("row", "col")),
            P("row", "col", None, None),
            P("row", "col", None),
            P("row", "col", None),
        ),
        out_specs=(P(None, ("row", "col")), P()),
        check_vma=False,
    )
```

```python
import math

import jax
import jax.numpy as jnp
from jax import lax
from jax.experimental import pallas as pl
from jax.experimental.pallas import tpu as pltpu
from jax.sharding import PartitionSpec as P

F32 = jnp.float32
BF16 = jnp.bfloat16


def limit(mib):
    return pltpu.CompilerParams(vmem_limit_bytes=mib << 20)


def hbm(value):
    return pltpu.with_memory_space_constraint(value, pltpu.HBM)


def vmem():
    return pl.BlockSpec(memory_space=pltpu.VMEM)


def smem():
    return pl.BlockSpec(memory_space=pltpu.SMEM)


def swap(value, row_mask, col_mask):
    rows, cols = lax.axis_size("row"), lax.axis_size("col")
    pairs = [(r * cols + c, (r ^ row_mask) * cols + (c ^ col_mask)) for r in range(rows) for c in range(cols)]
    return lax.ppermute(value, ("row", "col"), pairs)


def bits(size):
    out = []
    mask = 1
    while mask < size:
        out.append(mask)
        mask *= 2
    return out


def split3(value):
    high = value.astype(BF16)
    rest = value - high.astype(F32)
    mid = rest.astype(BF16)
    low = (rest - mid.astype(F32)).astype(BF16)
    return high, mid, low


def scale_kernel(basis_ref, degree_ref, left_ref, right_ref):
    half = left_ref.shape[1]
    inv_root = lax.rsqrt(degree_ref[...].astype(F32))
    scaled = (basis_ref[...].astype(F32) * inv_root).astype(BF16)
    left_ref[...] = scaled[:, :half]
    right_ref[...] = scaled[:, half:]


def load_kernel(per_piece, zero_at, column_in, live_in, panel_in, index_ref, panel_ref, column_ref, live_ref, sem):
    copies = [
        pltpu.make_async_copy(column_in, column_ref, sem.at[0]),
        pltpu.make_async_copy(live_in, live_ref, sem.at[1]),
        pltpu.make_async_copy(panel_in, panel_ref, sem.at[2]),
    ]
    for copy in copies:
        copy.start()
    copies[0].wait()
    copies[1].wait()
    column = column_ref[...] ^ (lax.axis_index("row") * per_piece)
    slot = lax.broadcasted_iota(jnp.int32, column.shape, 0)
    column = column ^ (slot & 1)
    index_ref[...] = jnp.where(live_ref[...] == 1, column, zero_at)
    copies[2].wait()


def tile_kernel(sources, groups, per_piece, left_order, right_order, index_ref, left_ref, right_ref,
                panel_ref, keep_ref, send_ref, table_ref, lhs_ref):
    vectors = left_ref.shape[1]
    half = left_ref.shape[2]
    height = panel_ref.shape[1]
    slots = index_ref.shape[0]
    wide = 2 * height
    pairs = half // wide
    my_col = lax.axis_index("col")
    zero_at = sources * per_piece
    for side, order, ref in ((0, left_order, left_ref), (1, right_order, right_ref)):
        for at in range(sources):
            for pair in range(pairs):
                tile = ref[at, :, pair * wide:(pair + 1) * wide]
                block = order[at] * per_piece + 2 * (side * pairs + pair)
                table_ref[block] = tile
                table_ref[block + 1] = jnp.concatenate([tile[:, height:], tile[:, :height]], axis=1)
    table_ref[zero_at] = jnp.zeros((vectors, wide), BF16)
    lane = lax.broadcasted_iota(jnp.int32, (vectors, wide), 1)
    is_low = lane < height
    pack = 4
    chunks = per_piece // pack

    def group(step, chunk, slot_of):
        partner = step & ~1
        flips = step & 1
        for bit in bits(groups)[1:]:
            flips = flips ^ ((step // bit) & 1)
        row0 = ((partner | flips) ^ my_col) * per_piece + chunk * pack
        for inner in range(pack):
            row = row0 + inner
            for pair in range(slots // 2):
                first = index_ref[2 * pair, row]
                second = index_ref[2 * pair + 1, row]
                lhs_ref[slot_of, inner * vectors:(inner + 1) * vectors, pair * wide:(pair + 1) * wide] = jnp.where(
                    is_low, table_ref[first], table_ref[second])
        rhs = panel_ref[pl.ds(row0, pack)].reshape(pack * height, slots * height)
        prod = lax.dot_general(lhs_ref[slot_of], rhs, (((1,), (1,)), ((), ())), preferred_element_type=F32)
        out = []
        for pair in range(pack // 2):
            lanes = slice(pair * wide, (pair + 1) * wide)
            top = prod[2 * pair * vectors:(2 * pair + 1) * vectors, lanes]
            low = prod[(2 * pair + 1) * vectors:(2 * pair + 2) * vectors, lanes]
            out.append(jnp.where(is_low, top, low))
        return jnp.concatenate(out, axis=1)

    span = pack * height
    if groups <= 4:
        at = 0
        for piece in [s for s in range(groups) if s % 2] + [s for s in range(groups) if s % 2 == 0]:
            for chunk in range(chunks):
                value = group(piece, chunk, at % 2)
                at += 1
                lanes = slice(chunk * span, (chunk + 1) * span)
                if piece % 2:
                    send_ref[piece // 2, :, lanes] = value.astype(BF16)
                else:
                    keep_ref[piece // 2, :, lanes] = value
    else:
        def body(step, carry):
            for chunk in range(chunks):
                lanes = slice(chunk * span, (chunk + 1) * span)
                send_ref[step, :, lanes] = group(2 * step + 1, chunk, 0).astype(BF16)
                keep_ref[step, :, lanes] = group(2 * step, chunk, 1)
            return carry

        lax.fori_loop(0, groups // 2, body, 0)


def gram_kernel(received, basis_ref, degree_ref, keep_ref, *refs):
    parts = refs[:received]
    split_ref, gram_ref, stack_ref = refs[received:]
    vectors = basis_ref.shape[0]
    spread = keep_ref[0]
    for ref in parts:
        spread = spread + ref[0].astype(F32)
    basis = basis_ref[...]
    inv_root = lax.rsqrt(degree_ref[...].astype(F32))
    applied = basis.astype(F32) - inv_root * spread
    for at, piece in enumerate(split3(applied)):
        split_ref[at * vectors:(at + 1) * vectors, :] = piece
        stack_ref[at * vectors:(at + 1) * vectors, :] = piece
    stack_ref[3 * vectors:4 * vectors, :] = basis
    stack = stack_ref[...]
    prod = lax.dot_general(stack, stack, (((1,), (1,)), ((), ())), preferred_element_type=F32)
    wide = 2 * vectors
    near = prod[:, :wide]
    far = prod[:, wide:]

    def rows(value, at):
        return value[at * vectors:(at + 1) * vectors]

    energy_low = rows(near, 0) + (rows(near, 1) + (rows(near, 2) + rows(far, 0)))
    energy_high = rows(near, 0) + rows(near, 1)
    quotient_low = rows(near, 3) + rows(far, 3)
    quotient_high = rows(near, 3)
    lane = lax.broadcasted_iota(jnp.int32, (vectors, wide), 1)
    gram_ref[...] = jnp.where(
        lane < vectors,
        energy_low + pltpu.roll(energy_high, vectors, 1),
        quotient_high + pltpu.roll(quotient_low, vectors, 1),
    )


def finish_kernel(total_rows, gram_ref, split_ref, out_ref, quotient_ref):
    vectors = gram_ref.shape[0]
    wide = 2 * vectors
    gram = gram_ref[...]
    quotient_ref[...] = (gram / total_rows)[:, vectors:]
    row = lax.broadcasted_iota(jnp.int32, (vectors, wide), 0)
    lane = lax.broadcasted_iota(jnp.int32, (vectors, wide), 1)
    work = jnp.where(lane < vectors, gram, jnp.where(lane == row + vectors, 1.0, 0.0))
    height = 8
    tiles = [work[at * height:(at + 1) * height] for at in range(vectors // height)]
    row8 = lax.broadcasted_iota(jnp.int32, (height, wide), 0)
    for step in range(vectors):
        home = step // height
        own = tiles[home][step % height:step % height + 1]
        scaled = own / own[:, step:step + 1]
        for at in range(home, vectors // height):
            column = tiles[at][:, step:step + 1]
            change = column * scaled
            if at == home:
                change = jnp.where(row8 > step % height, change, 0.0)
            tiles[at] = tiles[at] - change
    done = jnp.concatenate(tiles, axis=0)
    pivot = jnp.sum(jnp.where(lane == row, done, 0.0), axis=1, keepdims=True)
    inverse = done * (lax.rsqrt(pivot) * math.sqrt(total_rows))
    inverse = inverse[:, vectors:]
    w_high, w_mid, w_low = split3(inverse)
    left = jnp.concatenate([w_high, w_high, w_high, w_mid, w_mid, w_low], axis=1)
    pieces = split_ref[...]
    right = jnp.concatenate([pieces, pieces[:2 * vectors], pieces[:vectors]], axis=0)
    out_ref[...] = jnp.dot(left, right, preferred_element_type=F32)


def on_device(krylov_block, degree, tile_values, tile_column, tile_live):
    vectors, owned = krylov_block.shape
    block_rows, _, height, slot_width = tile_values.shape
    sources = lax.axis_size("row")
    groups = lax.axis_size("col")
    per_piece = owned // height
    half = owned // 2
    degree_row = degree.reshape(1, owned)
    left, right = pl.pallas_call(
        scale_kernel,
        out_shape=[jax.ShapeDtypeStruct((vectors, half), BF16)] * 2,
        in_specs=[vmem(), vmem()],
        out_specs=[vmem(), vmem()],
        compiler_params=limit(2),
        name="scale",
    )(hbm(krylov_block), hbm(degree_row))
    slots = tile_column.shape[2]
    index, panel = pl.pallas_call(
        lambda *refs: load_kernel(per_piece, sources * per_piece, *refs),
        out_shape=[
            jax.ShapeDtypeStruct((slots, block_rows), jnp.int32),
            jax.ShapeDtypeStruct((block_rows, height, slot_width), BF16),
        ],
        in_specs=[pl.BlockSpec(memory_space=pl.ANY)] * 3,
        out_specs=[vmem(), vmem()],
        scratch_shapes=[
            pltpu.VMEM((slots, block_rows), jnp.int32),
            pltpu.VMEM((slots, block_rows), jnp.int32),
            pltpu.SemaphoreType.DMA((3,)),
        ],
        compiler_params=limit(2),
        name="load",
    )(hbm(tile_column[:, 0].T), hbm(tile_live[:, 0].T), hbm(tile_values[:, 0]))
    row_bits = bits(sources)
    left_bits = row_bits[:0:-1] + row_bits[:1]
    right_bits = row_bits[:1] + row_bits[:0:-1]
    left, right = left[None], right[None]
    left_order, right_order = [0], [0]
    for left_bit, right_bit in zip(left_bits, right_bits):
        new_left = swap(left, left_bit, 0)
        new_right = swap(right, right_bit, 0)
        left = jnp.concatenate([left, new_left], axis=0)
        right = jnp.concatenate([right, new_right], axis=0)
        left_order = left_order + [at ^ left_bit for at in left_order]
        right_order = right_order + [at ^ right_bit for at in right_order]
    many = groups // 2
    keep, send = pl.pallas_call(
        lambda *refs: tile_kernel(sources, groups, per_piece, left_order, right_order, *refs),
        out_shape=[
            jax.ShapeDtypeStruct((many, vectors, owned), F32),
            jax.ShapeDtypeStruct((many, vectors, owned), BF16),
        ],
        in_specs=[smem(), vmem(), vmem(), vmem()],
        out_specs=[vmem(), vmem()],
        scratch_shapes=[
            pltpu.VMEM((sources * per_piece + 1, vectors, 2 * height), BF16),
            pltpu.VMEM((2, 4 * vectors, slot_width), BF16),
        ],
        compiler_params=limit(12),
        name="tiles",
    )(index, left, right, panel)
    running = keep
    received = []
    for bit in bits(groups):
        got = swap(send, 0, bit | 1)
        received.append(got)
        if running.shape[0] > 1:
            summed = running + got.astype(F32)
            pairs = summed.reshape((-1, 2) + summed.shape[1:])
            running, send = pairs[:, 0], pairs[:, 1].astype(BF16)
    pieces, gram = pl.pallas_call(
        lambda *refs: gram_kernel(len(received), *refs),
        out_shape=[
            jax.ShapeDtypeStruct((3 * vectors, owned), BF16),
            jax.ShapeDtypeStruct((vectors, 2 * vectors), F32),
        ],
        in_specs=[vmem()] * (3 + len(received)),
        out_specs=[vmem(), vmem()],
        scratch_shapes=[pltpu.VMEM((4 * vectors, owned), BF16)],
        compiler_params=limit(4),
        name="gram",
    )(krylov_block, degree_row, keep, *received)
    for bit in bits(groups):
        gram = gram + swap(gram, 0, bit | 1)
    for bit in bits(sources):
        gram = gram + swap(gram, bit, 1)
    total_rows = sources * groups * owned
    orthonormal, quotient = pl.pallas_call(
        lambda *refs: finish_kernel(total_rows, *refs),
        out_shape=[
            jax.ShapeDtypeStruct((vectors, owned), F32),
            jax.ShapeDtypeStruct((vectors, vectors), F32),
        ],
        in_specs=[vmem(), vmem()],
        out_specs=[vmem(), vmem()],
        compiler_params=limit(4),
        name="finish",
    )(gram, pieces)
    return (orthonormal, quotient)


def solution(mesh):
    return jax.shard_map(
        on_device,
        mesh=mesh,
        in_specs=(
            P(None, ("row", "col")),
            P(("row", "col")),
            P("row", "col", None, None),
            P("row", "col", None),
            P("row", "col", None),
        ),
        out_specs=(P(None, ("row", "col")), P()),
        check_vma=False,
    )
```

```python
import math

import jax
import jax.numpy as jnp
from jax import lax
from jax.experimental import pallas as pl
from jax.experimental.pallas import tpu as pltpu
from jax.sharding import PartitionSpec as P

F32 = jnp.float32
BF16 = jnp.bfloat16


def limit(mib):
    return pltpu.CompilerParams(vmem_limit_bytes=mib << 20)


def hbm(value):
    return pltpu.with_memory_space_constraint(value, pltpu.HBM)


def vmem():
    return pl.BlockSpec(memory_space=pltpu.VMEM)


def smem():
    return pl.BlockSpec(memory_space=pltpu.SMEM)


def swap(value, row_mask, col_mask):
    rows, cols = lax.axis_size("row"), lax.axis_size("col")
    pairs = [(r * cols + c, (r ^ row_mask) * cols + (c ^ col_mask)) for r in range(rows) for c in range(cols)]
    return lax.ppermute(value, ("row", "col"), pairs)


def bits(size):
    out = []
    mask = 1
    while mask < size:
        out.append(mask)
        mask *= 2
    return out


def split3(value):
    high = value.astype(BF16)
    rest = value - high.astype(F32)
    mid = rest.astype(BF16)
    low = (rest - mid.astype(F32)).astype(BF16)
    return high, mid, low


def scale_kernel(basis_ref, degree_ref, left_ref, right_ref, share_ref):
    vectors = basis_ref.shape[0]
    half = left_ref.shape[1]
    basis = basis_ref[...]
    degree = degree_ref[...].astype(F32)
    scaled = (basis.astype(F32) * lax.rsqrt(degree)).astype(BF16)
    left_ref[...] = scaled[:, :half]
    right_ref[...] = scaled[:, half:]
    share_ref[:vectors, :] = basis
    share_ref[vectors:, :] = jnp.broadcast_to(degree, (16, 2 * half)).astype(BF16)


def load_kernel(per_piece, zero_at, column_in, live_in, panel_in, index_ref, panel_ref, column_ref, live_ref, sem):
    copies = [
        pltpu.make_async_copy(column_in, column_ref, sem.at[0]),
        pltpu.make_async_copy(live_in, live_ref, sem.at[1]),
        pltpu.make_async_copy(panel_in, panel_ref, sem.at[2]),
    ]
    for copy in copies:
        copy.start()
    copies[0].wait()
    copies[1].wait()
    column = column_ref[...] ^ (lax.axis_index("row") * per_piece)
    slot = lax.broadcasted_iota(jnp.int32, column.shape, 0)
    column = column ^ (slot & 1)
    index_ref[...] = jnp.where(live_ref[...] == 1, column, zero_at)
    copies[2].wait()


def tile_kernel(sources, groups, per_piece, left_order, right_order, index_ref, left_ref, right_ref,
                panel_ref, keep_ref, send_ref, table_ref, lhs_ref):
    vectors = left_ref.shape[1]
    half = left_ref.shape[2]
    height = panel_ref.shape[1]
    slots = index_ref.shape[0]
    wide = 2 * height
    pairs = half // wide
    my_col = lax.axis_index("col")
    zero_at = sources * per_piece
    for side, order, ref in ((0, left_order, left_ref), (1, right_order, right_ref)):
        for at in range(sources):
            for pair in range(pairs):
                tile = ref[at, :, pair * wide:(pair + 1) * wide]
                block = order[at] * per_piece + 2 * (side * pairs + pair)
                table_ref[block] = tile
                table_ref[block + 1] = jnp.concatenate([tile[:, height:], tile[:, :height]], axis=1)
    table_ref[zero_at] = jnp.zeros((vectors, wide), BF16)
    lane = lax.broadcasted_iota(jnp.int32, (vectors, wide), 1)
    is_low = lane < height
    pack = 4
    chunks = per_piece // pack

    def group(step, chunk, slot_of):
        partner = step & ~1
        flips = step & 1
        for bit in bits(groups)[1:]:
            flips = flips ^ ((step // bit) & 1)
        row0 = ((partner | flips) ^ my_col) * per_piece + chunk * pack
        for inner in range(pack):
            row = row0 + inner
            for pair in range(slots // 2):
                first = index_ref[2 * pair, row]
                second = index_ref[2 * pair + 1, row]
                lhs_ref[slot_of, inner * vectors:(inner + 1) * vectors, pair * wide:(pair + 1) * wide] = jnp.where(
                    is_low, table_ref[first], table_ref[second])
        rhs = panel_ref[pl.ds(row0, pack)].reshape(pack * height, slots * height)
        prod = lax.dot_general(lhs_ref[slot_of], rhs, (((1,), (1,)), ((), ())), preferred_element_type=F32)
        out = []
        for pair in range(pack // 2):
            lanes = slice(pair * wide, (pair + 1) * wide)
            top = prod[2 * pair * vectors:(2 * pair + 1) * vectors, lanes]
            low = prod[(2 * pair + 1) * vectors:(2 * pair + 2) * vectors, lanes]
            out.append(jnp.where(is_low, top, low))
        return jnp.concatenate(out, axis=1)

    span = pack * height
    if groups <= 4:
        at = 0
        for piece in [s for s in range(groups) if s % 2] + [s for s in range(groups) if s % 2 == 0]:
            for chunk in range(chunks):
                value = group(piece, chunk, at % 2)
                at += 1
                lanes = slice(chunk * span, (chunk + 1) * span)
                if piece % 2:
                    send_ref[piece // 2, :, lanes] = value.astype(BF16)
                else:
                    keep_ref[piece // 2, :, lanes] = value
    else:
        def body(step, carry):
            for chunk in range(chunks):
                lanes = slice(chunk * span, (chunk + 1) * span)
                send_ref[step, :, lanes] = group(2 * step + 1, chunk, 0).astype(BF16)
                keep_ref[step, :, lanes] = group(2 * step, chunk, 1)
            return carry

        lax.fori_loop(0, groups // 2, body, 0)


def gram_kernel(last, mine_ref, theirs_ref, sums_ref, got_ref, split_ref, gram_ref, stack_ref):
    vectors = mine_ref.shape[0] - 16
    upper = (lax.axis_index("col") // last) & 1
    for place, share_ref in ((0, mine_ref), (1, theirs_ref)):
        basis = share_ref[:vectors, :]
        inv_root = lax.rsqrt(share_ref[vectors:, :].astype(F32))[:1]
        spread = sums_ref[place].astype(F32) + got_ref[1 - place].astype(F32)
        applied = basis.astype(F32) - inv_root * spread
        slot = upper if place == 0 else 1 - upper
        for at, piece in enumerate(split3(applied)):
            if place == 0:
                split_ref[at * vectors:(at + 1) * vectors, :] = piece
            stack_ref[slot, at * vectors:(at + 1) * vectors, :] = piece
        stack_ref[slot, 3 * vectors:4 * vectors, :] = basis
    dims = (((1,), (1,)), ((), ()))
    first, second = stack_ref[0], stack_ref[1]
    prod = lax.dot_general(first, first, dims, preferred_element_type=F32) + lax.dot_general(
        second, second, dims, preferred_element_type=F32)
    wide = 2 * vectors
    near = prod[:, :wide]
    far = prod[:, wide:]

    def rows(value, at):
        return value[at * vectors:(at + 1) * vectors]

    energy_low = rows(near, 0) + (rows(near, 1) + (rows(near, 2) + rows(far, 0)))
    energy_high = rows(near, 0) + rows(near, 1)
    quotient_low = rows(near, 3) + rows(far, 3)
    quotient_high = rows(near, 3)
    lane = lax.broadcasted_iota(jnp.int32, (vectors, wide), 1)
    gram_ref[...] = jnp.where(
        lane < vectors,
        energy_low + pltpu.roll(energy_high, vectors, 1),
        quotient_high + pltpu.roll(quotient_low, vectors, 1),
    )


def finish_kernel(total_rows, gram_ref, split_ref, out_ref, quotient_ref):
    vectors = gram_ref.shape[0]
    wide = 2 * vectors
    gram = gram_ref[...]
    quotient_ref[...] = (gram / total_rows)[:, vectors:]
    row = lax.broadcasted_iota(jnp.int32, (vectors, wide), 0)
    lane = lax.broadcasted_iota(jnp.int32, (vectors, wide), 1)
    work = jnp.where(lane < vectors, gram, jnp.where(lane == row + vectors, 1.0, 0.0))
    height = 8
    tiles = [work[at * height:(at + 1) * height] for at in range(vectors // height)]
    below = lax.broadcasted_iota(jnp.int32, (height, wide), 0)

    def across(tile, at):
        return jnp.broadcast_to(tile[:, at:at + 1], (height, wide))

    def down(tile, at):
        return jnp.broadcast_to(tile[at:at + 1], (height, wide))

    for home in range(len(tiles)):
        columns = [[across(tile, home * height + at) for at in range(height)] for tile in tiles[home:]]
        for at in range(height):
            own = columns[0]
            scale = 1.0 / down(own[at], at)
            pivot_row = down(tiles[home], at)
            entries = [down(own[later], at) for later in range(height)]
            for place, column in enumerate(columns):
                factor = column[at] * scale
                if place == 0:
                    factor = jnp.where(below > at, factor, 0.0)
                tiles[home + place] = tiles[home + place] - factor * pivot_row
                for later in range(at + 1, height):
                    column[later] = column[later] - factor * entries[later]
    done = jnp.concatenate(tiles, axis=0)
    pivot = jnp.sum(jnp.where(lane == row, done, 0.0), axis=1, keepdims=True)
    inverse = done * (lax.rsqrt(pivot) * math.sqrt(total_rows))
    inverse = inverse[:, vectors:]
    w_high, w_mid, w_low = split3(inverse)
    left = jnp.concatenate([w_high, w_high, w_high, w_mid, w_mid, w_low], axis=1)
    pieces = split_ref[...]
    right = jnp.concatenate([pieces, pieces[:2 * vectors], pieces[:vectors]], axis=0)
    out_ref[...] = jnp.dot(left, right, preferred_element_type=F32)


def on_device(krylov_block, degree, tile_values, tile_column, tile_live):
    vectors, owned = krylov_block.shape
    block_rows, _, height, slot_width = tile_values.shape
    sources = lax.axis_size("row")
    groups = lax.axis_size("col")
    per_piece = owned // height
    half = owned // 2
    degree_row = degree.reshape(1, owned)
    left, right, share = pl.pallas_call(
        scale_kernel,
        out_shape=[
            jax.ShapeDtypeStruct((vectors, half), BF16),
            jax.ShapeDtypeStruct((vectors, half), BF16),
            jax.ShapeDtypeStruct((vectors + 16, owned), BF16),
        ],
        in_specs=[vmem(), vmem()],
        out_specs=[vmem(), vmem(), vmem()],
        compiler_params=limit(2),
        name="scale",
    )(hbm(krylov_block), hbm(degree_row))
    slots = tile_column.shape[2]
    index, panel = pl.pallas_call(
        lambda *refs: load_kernel(per_piece, sources * per_piece, *refs),
        out_shape=[
            jax.ShapeDtypeStruct((slots, block_rows), jnp.int32),
            jax.ShapeDtypeStruct((block_rows, height, slot_width), BF16),
        ],
        in_specs=[pl.BlockSpec(memory_space=pl.ANY)] * 3,
        out_specs=[vmem(), vmem()],
        scratch_shapes=[
            pltpu.VMEM((slots, block_rows), jnp.int32),
            pltpu.VMEM((slots, block_rows), jnp.int32),
            pltpu.SemaphoreType.DMA((3,)),
        ],
        compiler_params=limit(2),
        name="load",
    )(hbm(tile_column[:, 0].T), hbm(tile_live[:, 0].T), hbm(tile_values[:, 0]))
    row_bits = bits(sources)
    left_bits = row_bits[:0:-1] + row_bits[:1]
    right_bits = row_bits[:1] + row_bits[:0:-1]
    left, right = left[None], right[None]
    left_order, right_order = [0], [0]
    for left_bit, right_bit in zip(left_bits, right_bits):
        new_left = swap(left, left_bit, 0)
        new_right = swap(right, right_bit, 0)
        if left_bit == left_bits[0]:
            new_left, share = lax.optimization_barrier((new_left, share))
            other_share = swap(share, 0, bits(groups)[-1] | 1)
        elif left_bit == left_bits[-1]:
            new_left, other_share = lax.optimization_barrier((new_left, other_share))
        left = jnp.concatenate([left, new_left], axis=0)
        right = jnp.concatenate([right, new_right], axis=0)
        left_order = left_order + [at ^ left_bit for at in left_order]
        right_order = right_order + [at ^ right_bit for at in right_order]
    many = groups // 2
    keep, send = pl.pallas_call(
        lambda *refs: tile_kernel(sources, groups, per_piece, left_order, right_order, *refs),
        out_shape=[
            jax.ShapeDtypeStruct((many, vectors, owned), F32),
            jax.ShapeDtypeStruct((many, vectors, owned), BF16),
        ],
        in_specs=[smem(), vmem(), vmem(), vmem()],
        out_specs=[vmem(), vmem()],
        scratch_shapes=[
            pltpu.VMEM((sources * per_piece + 1, vectors, 2 * height), BF16),
            pltpu.VMEM((2, 4 * vectors, slot_width), BF16),
        ],
        compiler_params=limit(12),
        name="tiles",
    )(index, left, right, panel)
    col_bits = bits(groups)
    last = col_bits.pop()
    for bit in col_bits:
        summed = keep + swap(send, 0, bit | 1).astype(F32)
        if bit != col_bits[-1]:
            pairs = summed.reshape((-1, 2) + summed.shape[1:])
            keep, send = pairs[:, 0], pairs[:, 1].astype(BF16)
    sums = summed.astype(BF16)
    got = swap(sums, 0, last | 1)
    pieces, gram = pl.pallas_call(
        lambda *refs: gram_kernel(last, *refs),
        out_shape=[
            jax.ShapeDtypeStruct((3 * vectors, owned), BF16),
            jax.ShapeDtypeStruct((vectors, 2 * vectors), F32),
        ],
        in_specs=[vmem()] * 4,
        out_specs=[vmem(), vmem()],
        scratch_shapes=[pltpu.VMEM((2, 4 * vectors, owned), BF16)],
        compiler_params=limit(4),
        name="gram",
    )(share, other_share, sums, got)
    for bit in col_bits:
        gram = gram + swap(gram, 0, bit | 1)
    for bit in bits(sources):
        gram = gram + swap(gram, bit, 1)
    total_rows = sources * groups * owned
    orthonormal, quotient = pl.pallas_call(
        lambda *refs: finish_kernel(total_rows, *refs),
        out_shape=[
            jax.ShapeDtypeStruct((vectors, owned), F32),
            jax.ShapeDtypeStruct((vectors, vectors), F32),
        ],
        in_specs=[vmem(), vmem()],
        out_specs=[vmem(), vmem()],
        compiler_params=limit(4),
        name="finish",
    )(gram, pieces)
    return (orthonormal, quotient)


def solution(mesh):
    return jax.shard_map(
        on_device,
        mesh=mesh,
        in_specs=(
            P(None, ("row", "col")),
            P(("row", "col")),
            P("row", "col", None, None),
            P("row", "col", None),
            P("row", "col", None),
        ),
        out_specs=(P(None, ("row", "col")), P()),
        check_vma=False,
    )
```

```python
import math

import jax
import jax.numpy as jnp
from jax import lax
from jax.experimental import pallas as pl
from jax.experimental.pallas import tpu as pltpu
from jax.sharding import PartitionSpec as P

F32 = jnp.float32
BF16 = jnp.bfloat16


def limit(mib):
    return pltpu.CompilerParams(vmem_limit_bytes=mib << 20)


def hbm(value):
    return pltpu.with_memory_space_constraint(value, pltpu.HBM)


def vmem():
    return pl.BlockSpec(memory_space=pltpu.VMEM)


def smem():
    return pl.BlockSpec(memory_space=pltpu.SMEM)


def swap(value, row_mask, col_mask):
    rows, cols = lax.axis_size("row"), lax.axis_size("col")
    pairs = [(r * cols + c, (r ^ row_mask) * cols + (c ^ col_mask)) for r in range(rows) for c in range(cols)]
    return lax.ppermute(value, ("row", "col"), pairs)


def bits(size):
    out = []
    mask = 1
    while mask < size:
        out.append(mask)
        mask *= 2
    return out


def split3(value):
    high = value.astype(BF16)
    rest = value - high.astype(F32)
    mid = rest.astype(BF16)
    low = (rest - mid.astype(F32)).astype(BF16)
    return high, mid, low


def scale_kernel(basis_ref, degree_ref, scaled_ref, share_ref):
    vectors, owned = basis_ref.shape
    basis = basis_ref[...]
    degree = degree_ref[...].astype(F32)
    scaled_ref[...] = (basis.astype(F32) * lax.rsqrt(degree)).astype(BF16)
    share_ref[:vectors, :] = basis
    share_ref[vectors:, :] = jnp.broadcast_to(degree, (16, owned)).astype(BF16)


def fill_table(table_ref, per_piece, height, orders, refs):
    wide = 2 * height
    pairs = refs[0].shape[2] // wide
    for side, (order, ref) in enumerate(zip(orders, refs)):
        for at, source in enumerate(order):
            for pair in range(pairs):
                tile = ref[at, :, pair * wide:(pair + 1) * wide]
                block = source * per_piece + 2 * (side * pairs + pair)
                table_ref[block] = tile
                table_ref[block + 1] = jnp.concatenate([tile[:, height:], tile[:, :height]], axis=1)


def load_kernel(per_piece, zero_at, orders, column_in, live_in, panel_in, left_ref, right_ref, index_ref, panel_ref,
                table_ref, column_ref, live_ref, work_ref, sem):
    copies = [
        pltpu.make_async_copy(column_in, column_ref, sem.at[0]),
        pltpu.make_async_copy(live_in, live_ref, sem.at[1]),
        pltpu.make_async_copy(panel_in, panel_ref, sem.at[2]),
    ]
    for copy in copies:
        copy.start()
    fill_table(table_ref, per_piece, panel_ref.shape[1], orders, (left_ref, right_ref))
    table_ref[zero_at] = jnp.zeros(table_ref.shape[1:], BF16)
    copies[0].wait()
    copies[1].wait()
    column = column_ref[...] ^ (lax.axis_index("row") * per_piece)
    slot = lax.broadcasted_iota(jnp.int32, column.shape, 0)
    column = column ^ (slot & 1)
    work_ref[...] = jnp.where(live_ref[...] == 1, column, zero_at)
    last = pltpu.make_async_copy(work_ref, index_ref, sem.at[3])
    last.start()
    copies[2].wait()
    last.wait()


def multiply(groups, per_piece, odd, index_ref, panel_ref, table_ref, lhs_ref, out_ref):
    height = panel_ref.shape[1]
    slots = index_ref.shape[0]
    vectors = table_ref.shape[1]
    wide = 2 * height
    my_col = lax.axis_index("col")
    is_low = lax.broadcasted_iota(jnp.int32, (vectors, wide), 1) < height
    pack = 4
    span = pack * height

    def chunk_of(step, chunk):
        flips = odd
        for bit in bits(groups)[:-1]:
            flips = flips ^ ((step // bit) & 1)
        row0 = ((2 * step + flips) ^ my_col) * per_piece + chunk * pack
        slot_of = chunk % 2
        for inner in range(pack):
            row = row0 + inner
            for pair in range(slots // 2):
                first = index_ref[2 * pair, row]
                second = index_ref[2 * pair + 1, row]
                lhs_ref[slot_of, inner * vectors:(inner + 1) * vectors, pair * wide:(pair + 1) * wide] = jnp.where(
                    is_low, table_ref[first], table_ref[second])
        rhs = panel_ref[pl.ds(row0, pack)].reshape(pack * height, slots * height)
        prod = lax.dot_general(lhs_ref[slot_of], rhs, (((1,), (1,)), ((), ())), preferred_element_type=F32)
        for pair in range(pack // 2):
            lanes = slice(pair * wide, (pair + 1) * wide)
            top = prod[2 * pair * vectors:(2 * pair + 1) * vectors, lanes]
            low = prod[(2 * pair + 1) * vectors:(2 * pair + 2) * vectors, lanes]
            at = chunk * span + pair * wide
            out_ref[step, :, at:at + wide] = jnp.where(is_low, top, low).astype(out_ref.dtype)

    if groups <= 4:
        for step in range(groups // 2):
            for chunk in range(per_piece // pack):
                chunk_of(step, chunk)
    else:
        def body(step, carry):
            for chunk in range(per_piece // pack):
                chunk_of(step, chunk)
            return carry

        lax.fori_loop(0, groups // 2, body, 0)


def send_kernel(groups, per_piece, orders, index_ref, panel_ref, table_in, left_ref, right_ref, table_ref, send_ref,
                lhs_ref):
    del table_in
    fill_table(table_ref, per_piece, panel_ref.shape[1], orders, (left_ref, right_ref))
    multiply(groups, per_piece, 1, index_ref, panel_ref, table_ref, lhs_ref, send_ref)


def keep_kernel(groups, per_piece, index_ref, panel_ref, table_ref, keep_ref, lhs_ref):
    multiply(groups, per_piece, 0, index_ref, panel_ref, table_ref, lhs_ref, keep_ref)


def gram_kernel(last, mine_ref, theirs_ref, sums_ref, got_ref, split_ref, gram_ref, stack_ref):
    vectors = mine_ref.shape[0] - 16
    upper = (lax.axis_index("col") // last) & 1
    for place, share_ref in ((0, mine_ref), (1, theirs_ref)):
        basis = share_ref[:vectors, :]
        inv_root = lax.rsqrt(share_ref[vectors:, :].astype(F32))[:1]
        spread = sums_ref[place].astype(F32) + got_ref[1 - place].astype(F32)
        applied = basis.astype(F32) - inv_root * spread
        slot = upper if place == 0 else 1 - upper
        for at, piece in enumerate(split3(applied)):
            if place == 0:
                split_ref[at * vectors:(at + 1) * vectors, :] = piece
            stack_ref[slot, at * vectors:(at + 1) * vectors, :] = piece
        stack_ref[slot, 3 * vectors:4 * vectors, :] = basis
    dims = (((1,), (1,)), ((), ()))
    first, second = stack_ref[0], stack_ref[1]
    prod = lax.dot_general(first, first, dims, preferred_element_type=F32) + lax.dot_general(
        second, second, dims, preferred_element_type=F32)
    wide = 2 * vectors
    near = prod[:, :wide]
    far = prod[:, wide:]

    def rows(value, at):
        return value[at * vectors:(at + 1) * vectors]

    energy_low = rows(near, 0) + (rows(near, 1) + (rows(near, 2) + rows(far, 0)))
    energy_high = rows(near, 0) + rows(near, 1)
    quotient_low = rows(near, 3) + rows(far, 3)
    quotient_high = rows(near, 3)
    lane = lax.broadcasted_iota(jnp.int32, (vectors, wide), 1)
    gram_ref[...] = jnp.where(
        lane < vectors,
        energy_low + pltpu.roll(energy_high, vectors, 1),
        quotient_high + pltpu.roll(quotient_low, vectors, 1),
    )


def finish_kernel(total_rows, gram_ref, split_ref, out_ref, quotient_ref):
    vectors = gram_ref.shape[0]
    wide = 2 * vectors
    gram = gram_ref[...]
    quotient_ref[...] = (gram / total_rows)[:, vectors:]
    row = lax.broadcasted_iota(jnp.int32, (vectors, wide), 0)
    lane = lax.broadcasted_iota(jnp.int32, (vectors, wide), 1)
    work = jnp.where(lane < vectors, gram, jnp.where(lane == row + vectors, 1.0, 0.0))
    height = 8
    tiles = [work[at * height:(at + 1) * height] for at in range(vectors // height)]
    below = lax.broadcasted_iota(jnp.int32, (height, wide), 0)

    def across(tile, at):
        return jnp.broadcast_to(tile[:, at:at + 1], (height, wide))

    def down(tile, at):
        return jnp.broadcast_to(tile[at:at + 1], (height, wide))

    for home in range(len(tiles)):
        columns = [[across(tile, home * height + at) for at in range(height)] for tile in tiles[home:]]
        for at in range(height):
            own = columns[0]
            scale = 1.0 / down(own[at], at)
            pivot_row = down(tiles[home], at)
            entries = [down(own[later], at) for later in range(height)]
            for place, column in enumerate(columns):
                factor = column[at] * scale
                if place == 0:
                    factor = jnp.where(below > at, factor, 0.0)
                tiles[home + place] = tiles[home + place] - factor * pivot_row
                for later in range(at + 1, height):
                    column[later] = column[later] - factor * entries[later]
    done = jnp.concatenate(tiles, axis=0)
    pivot = jnp.sum(jnp.where(lane == row, done, 0.0), axis=1, keepdims=True)
    inverse = done * (lax.rsqrt(pivot) * math.sqrt(total_rows))
    inverse = inverse[:, vectors:]
    w_high, w_mid, w_low = split3(inverse)
    left = jnp.concatenate([w_high, w_high, w_high, w_mid, w_mid, w_low], axis=1)
    pieces = split_ref[...]
    right = jnp.concatenate([pieces, pieces[:2 * vectors], pieces[:vectors]], axis=0)
    out_ref[...] = jnp.dot(left, right, preferred_element_type=F32)


def on_device(krylov_block, degree, tile_values, tile_column, tile_live):
    vectors, owned = krylov_block.shape
    block_rows, _, height, slot_width = tile_values.shape
    sources = lax.axis_size("row")
    groups = lax.axis_size("col")
    per_piece = owned // height
    half = owned // 2
    degree_row = degree.reshape(1, owned)
    scaled, share = pl.pallas_call(
        scale_kernel,
        out_shape=[
            jax.ShapeDtypeStruct((vectors, owned), BF16),
            jax.ShapeDtypeStruct((vectors + 16, owned), BF16),
        ],
        in_specs=[vmem(), vmem()],
        out_specs=[vmem(), vmem()],
        compiler_params=limit(2),
        name="scale",
    )(hbm(krylov_block), hbm(degree_row))
    row_bits = bits(sources)
    top = row_bits.pop()
    other = swap(scaled, top, 0)
    other_share = swap(share, 0, bits(groups)[-1] | 1)
    other, other_share = lax.optimization_barrier((other, other_share))
    left = jnp.stack([scaled[:, :half], other[:, :half]])
    right = jnp.stack([scaled[:, half:], other[:, half:]])
    left_order, right_order = [0, top], [0, top]
    for left_bit, right_bit in zip(row_bits[::-1], row_bits):
        if left_bit != row_bits[-1]:
            left = jnp.concatenate([left, new_left], axis=0)
            right = jnp.concatenate([right, new_right], axis=0)
        early = (left_order, right_order)
        new_left = swap(left, left_bit, 0)
        new_right = swap(right, right_bit, 0)
        late = ([at ^ left_bit for at in left_order], [at ^ right_bit for at in right_order])
        left_order = left_order + late[0]
        right_order = right_order + late[1]
    slots = tile_column.shape[2]
    many = groups // 2
    table_shape = (sources * per_piece + 1, vectors, 2 * height)
    index, panel, table = pl.pallas_call(
        lambda *refs: load_kernel(per_piece, sources * per_piece, early, *refs),
        out_shape=[
            pltpu.SMEM((slots, block_rows), jnp.int32),
            jax.ShapeDtypeStruct((block_rows, height, slot_width), BF16),
            jax.ShapeDtypeStruct(table_shape, BF16),
        ],
        in_specs=[pl.BlockSpec(memory_space=pl.ANY)] * 3 + [vmem()] * 2,
        out_specs=[smem(), vmem(), vmem()],
        scratch_shapes=[
            pltpu.VMEM((slots, block_rows), jnp.int32),
            pltpu.VMEM((slots, block_rows), jnp.int32),
            pltpu.VMEM((slots, block_rows), jnp.int32),
            pltpu.SemaphoreType.DMA((4,)),
        ],
        compiler_params=limit(2),
        name="load",
    )(hbm(tile_column[:, 0].T), hbm(tile_live[:, 0].T), hbm(tile_values[:, 0]), left, right)
    index = pltpu.with_memory_space_constraint(index, pltpu.SMEM)
    lhs = pltpu.VMEM((2, 4 * vectors, slot_width), BF16)
    table, send = pl.pallas_call(
        lambda *refs: send_kernel(groups, per_piece, late, *refs),
        out_shape=[
            jax.ShapeDtypeStruct(table_shape, BF16),
            jax.ShapeDtypeStruct((many, vectors, owned), BF16),
        ],
        in_specs=[smem()] + [vmem()] * 4,
        out_specs=[vmem(), vmem()],
        scratch_shapes=[lhs],
        input_output_aliases={2: 0},
        compiler_params=limit(8),
        name="send",
    )(index, panel, table, new_left, new_right)
    keep = pl.pallas_call(
        lambda *refs: keep_kernel(groups, per_piece, *refs),
        out_shape=jax.ShapeDtypeStruct((many, vectors, owned), F32),
        in_specs=[smem(), vmem(), vmem()],
        out_specs=vmem(),
        scratch_shapes=[lhs],
        compiler_params=limit(8),
        name="keep",
    )(index, panel, table)
    col_bits = bits(groups)
    last = col_bits.pop()
    for bit in col_bits:
        summed = keep + swap(send, 0, bit | 1).astype(F32)
        if bit != col_bits[-1]:
            pairs = summed.reshape((-1, 2) + summed.shape[1:])
            keep, send = pairs[:, 0], pairs[:, 1].astype(BF16)
    sums = summed.astype(BF16)
    got = swap(sums, 0, last | 1)
    pieces, gram = pl.pallas_call(
        lambda *refs: gram_kernel(last, *refs),
        out_shape=[
            jax.ShapeDtypeStruct((3 * vectors, owned), BF16),
            jax.ShapeDtypeStruct((vectors, 2 * vectors), F32),
        ],
        in_specs=[vmem()] * 4,
        out_specs=[vmem(), vmem()],
        scratch_shapes=[pltpu.VMEM((2, 4 * vectors, owned), BF16)],
        compiler_params=limit(4),
        name="gram",
    )(share, other_share, sums, got)
    for bit in col_bits:
        gram = gram + swap(gram, 0, bit | 1)
    for bit in bits(sources):
        gram = gram + swap(gram, bit, 1)
    total_rows = sources * groups * owned
    orthonormal, quotient = pl.pallas_call(
        lambda *refs: finish_kernel(total_rows, *refs),
        out_shape=[
            jax.ShapeDtypeStruct((vectors, owned), F32),
            jax.ShapeDtypeStruct((vectors, vectors), F32),
        ],
        in_specs=[vmem(), vmem()],
        out_specs=[vmem(), vmem()],
        compiler_params=limit(4),
        name="finish",
    )(gram, pieces)
    return (orthonormal, quotient)


def solution(mesh):
    return jax.shard_map(
        on_device,
        mesh=mesh,
        in_specs=(
            P(None, ("row", "col")),
            P(("row", "col")),
            P("row", "col", None, None),
            P("row", "col", None),
            P("row", "col", None),
        ),
        out_specs=(P(None, ("row", "col")), P()),
        check_vma=False,
    )
```

```python
import math

import jax
import jax.numpy as jnp
from jax import lax
from jax.experimental import pallas as pl
from jax.experimental.pallas import tpu as pltpu
from jax.sharding import PartitionSpec as P

F32 = jnp.float32
BF16 = jnp.bfloat16


def limit(mib):
    return pltpu.CompilerParams(vmem_limit_bytes=mib << 20)


def hbm(value):
    return pltpu.with_memory_space_constraint(value, pltpu.HBM)


def vmem():
    return pl.BlockSpec(memory_space=pltpu.VMEM)


def smem():
    return pl.BlockSpec(memory_space=pltpu.SMEM)


def swap(value, row_mask, col_mask):
    rows, cols = lax.axis_size("row"), lax.axis_size("col")
    pairs = [(r * cols + c, (r ^ row_mask) * cols + (c ^ col_mask)) for r in range(rows) for c in range(cols)]
    return lax.ppermute(value, ("row", "col"), pairs)


def bits(size):
    out = []
    mask = 1
    while mask < size:
        out.append(mask)
        mask *= 2
    return out


def split3(value):
    high = value.astype(BF16)
    rest = value - high.astype(F32)
    mid = rest.astype(BF16)
    low = (rest - mid.astype(F32)).astype(BF16)
    return high, mid, low


def scale_kernel(basis_ref, degree_ref, scaled_ref, share_ref):
    vectors, owned = basis_ref.shape
    basis = basis_ref[...]
    degree = degree_ref[...].astype(F32)
    scaled_ref[...] = (basis.astype(F32) * lax.rsqrt(degree)).astype(BF16)
    share_ref[:vectors, :] = basis
    share_ref[vectors:, :] = jnp.broadcast_to(degree, (16, owned)).astype(BF16)


def fill_table(table_ref, per_piece, height, sources, tiles_of):
    wide = 2 * height
    for source, ref in zip(sources, tiles_of):
        for pair in range(per_piece // 2):
            tile = ref[:, pair * wide:(pair + 1) * wide]
            block = source * per_piece + 2 * pair
            table_ref[block] = tile
            table_ref[block + 1] = jnp.concatenate([tile[:, height:], tile[:, :height]], axis=1)


def load_kernel(per_piece, zero_at, order, column_in, live_in, panel_in, near_ref, index_ref, panel_ref,
                table_ref, column_ref, live_ref, work_ref, sem):
    copies = [
        pltpu.make_async_copy(column_in, column_ref, sem.at[0]),
        pltpu.make_async_copy(live_in, live_ref, sem.at[1]),
        pltpu.make_async_copy(panel_in, panel_ref, sem.at[2]),
    ]
    for copy in copies:
        copy.start()
    fill_table(table_ref, per_piece, panel_ref.shape[1], order, [near_ref.at[at] for at in range(len(order))])
    table_ref[zero_at] = jnp.zeros(table_ref.shape[1:], BF16)
    copies[0].wait()
    copies[1].wait()
    column = column_ref[...] ^ (lax.axis_index("row") * per_piece)
    slot = lax.broadcasted_iota(jnp.int32, column.shape, 0)
    column = column ^ (slot & 1)
    work_ref[...] = jnp.where(live_ref[...] == 1, column, zero_at)
    last = pltpu.make_async_copy(work_ref, index_ref, sem.at[3])
    last.start()
    copies[2].wait()
    last.wait()


def multiply(groups, per_piece, odd, index_ref, panel_ref, table_ref, lhs_ref, out_ref):
    height = panel_ref.shape[1]
    slots = index_ref.shape[0]
    vectors = table_ref.shape[1]
    wide = 2 * height
    my_col = lax.axis_index("col")
    is_low = lax.broadcasted_iota(jnp.int32, (vectors, wide), 1) < height
    pack = 4
    span = pack * height

    def chunk_of(step, chunk):
        flips = odd
        for bit in bits(groups)[:-1]:
            flips = flips ^ ((step // bit) & 1)
        row0 = ((2 * step + flips) ^ my_col) * per_piece + chunk * pack
        slot_of = chunk % 2
        for inner in range(pack):
            row = row0 + inner
            for pair in range(slots // 2):
                first = index_ref[2 * pair, row]
                second = index_ref[2 * pair + 1, row]
                lhs_ref[slot_of, inner * vectors:(inner + 1) * vectors, pair * wide:(pair + 1) * wide] = jnp.where(
                    is_low, table_ref[first], table_ref[second])
        rhs = panel_ref[pl.ds(row0, pack)].reshape(pack * height, slots * height)
        prod = lax.dot_general(lhs_ref[slot_of], rhs, (((1,), (1,)), ((), ())), preferred_element_type=F32)
        for pair in range(pack // 2):
            lanes = slice(pair * wide, (pair + 1) * wide)
            top = prod[2 * pair * vectors:(2 * pair + 1) * vectors, lanes]
            low = prod[(2 * pair + 1) * vectors:(2 * pair + 2) * vectors, lanes]
            at = chunk * span + pair * wide
            out_ref[step, :, at:at + wide] = jnp.where(is_low, top, low).astype(out_ref.dtype)

    if groups <= 4:
        for step in range(groups // 2):
            for chunk in range(per_piece // pack):
                chunk_of(step, chunk)
    else:
        def body(step, carry):
            for chunk in range(per_piece // pack):
                chunk_of(step, chunk)
            return carry

        lax.fori_loop(0, groups // 2, body, 0)


def send_kernel(groups, per_piece, orders, index_ref, panel_ref, table_in, *refs):
    table_ref, send_ref, lhs_ref = refs[len(orders):]
    for order, ref in zip(orders, refs):
        fill_table(table_ref, per_piece, panel_ref.shape[1], order, [ref.at[at] for at in range(len(order))])
    multiply(groups, per_piece, 1, index_ref, panel_ref, table_ref, lhs_ref, send_ref)


def keep_kernel(groups, per_piece, index_ref, panel_ref, table_ref, keep_ref, lhs_ref):
    multiply(groups, per_piece, 0, index_ref, panel_ref, table_ref, lhs_ref, keep_ref)


def gram_kernel(last, mine_ref, theirs_ref, sums_ref, got_ref, split_ref, gram_ref, stack_ref):
    vectors = mine_ref.shape[0] - 16
    upper = (lax.axis_index("col") // last) & 1
    for place, share_ref in ((0, mine_ref), (1, theirs_ref)):
        basis = share_ref[:vectors, :]
        inv_root = lax.rsqrt(share_ref[vectors:, :].astype(F32))[:1]
        spread = sums_ref[place].astype(F32) + got_ref[1 - place].astype(F32)
        applied = basis.astype(F32) - inv_root * spread
        slot = upper if place == 0 else 1 - upper
        for at, piece in enumerate(split3(applied)):
            if place == 0:
                split_ref[at * vectors:(at + 1) * vectors, :] = piece
            stack_ref[slot, at * vectors:(at + 1) * vectors, :] = piece
        stack_ref[slot, 3 * vectors:4 * vectors, :] = basis
    dims = (((1,), (1,)), ((), ()))
    first, second = stack_ref[0], stack_ref[1]
    prod = lax.dot_general(first, first, dims, preferred_element_type=F32) + lax.dot_general(
        second, second, dims, preferred_element_type=F32)
    wide = 2 * vectors
    near = prod[:, :wide]
    far = prod[:, wide:]

    def rows(value, at):
        return value[at * vectors:(at + 1) * vectors]

    energy_low = rows(near, 0) + (rows(near, 1) + (rows(near, 2) + rows(far, 0)))
    energy_high = rows(near, 0) + rows(near, 1)
    quotient_low = rows(near, 3) + rows(far, 3)
    quotient_high = rows(near, 3)
    lane = lax.broadcasted_iota(jnp.int32, (vectors, wide), 1)
    gram_ref[...] = jnp.where(
        lane < vectors,
        energy_low + pltpu.roll(energy_high, vectors, 1),
        quotient_high + pltpu.roll(quotient_low, vectors, 1),
    )


def finish_kernel(total_rows, gram_ref, split_ref, out_ref, quotient_ref):
    vectors = gram_ref.shape[0]
    wide = 2 * vectors
    gram = gram_ref[...]
    quotient_ref[...] = (gram / total_rows)[:, vectors:]
    row = lax.broadcasted_iota(jnp.int32, (vectors, wide), 0)
    lane = lax.broadcasted_iota(jnp.int32, (vectors, wide), 1)
    work = jnp.where(lane < vectors, gram, jnp.where(lane == row + vectors, 1.0, 0.0))
    height = 8
    tiles = [work[at * height:(at + 1) * height] for at in range(vectors // height)]
    below = lax.broadcasted_iota(jnp.int32, (height, wide), 0)

    def across(tile, at):
        return jnp.broadcast_to(tile[:, at:at + 1], (height, wide))

    def down(tile, at):
        return jnp.broadcast_to(tile[at:at + 1], (height, wide))

    for home in range(len(tiles)):
        columns = [[across(tile, home * height + at) for at in range(height)] for tile in tiles[home:]]
        for at in range(height):
            own = columns[0]
            scale = 1.0 / down(own[at], at)
            pivot_row = down(tiles[home], at)
            entries = [down(own[later], at) for later in range(height)]
            for place, column in enumerate(columns):
                factor = column[at] * scale
                if place == 0:
                    factor = jnp.where(below > at, factor, 0.0)
                tiles[home + place] = tiles[home + place] - factor * pivot_row
                for later in range(at + 1, height):
                    column[later] = column[later] - factor * entries[later]
    done = jnp.concatenate(tiles, axis=0)
    pivot = jnp.sum(jnp.where(lane == row, done, 0.0), axis=1, keepdims=True)
    inverse = done * (lax.rsqrt(pivot) * math.sqrt(total_rows))
    inverse = inverse[:, vectors:]
    w_high, w_mid, w_low = split3(inverse)
    left = jnp.concatenate([w_high, w_high, w_high, w_mid, w_mid, w_low], axis=1)
    pieces = split_ref[...]
    right = jnp.concatenate([pieces, pieces[:2 * vectors], pieces[:vectors]], axis=0)
    out_ref[...] = jnp.dot(left, right, preferred_element_type=F32)


def on_device(krylov_block, degree, tile_values, tile_column, tile_live):
    vectors, owned = krylov_block.shape
    block_rows, _, height, slot_width = tile_values.shape
    sources = lax.axis_size("row")
    groups = lax.axis_size("col")
    per_piece = owned // height
    degree_row = degree.reshape(1, owned)
    scaled, share = pl.pallas_call(
        scale_kernel,
        out_shape=[
            jax.ShapeDtypeStruct((vectors, owned), BF16),
            jax.ShapeDtypeStruct((vectors + 16, owned), BF16),
        ],
        in_specs=[vmem(), vmem()],
        out_specs=[vmem(), vmem()],
        compiler_params=limit(2),
        name="scale",
    )(hbm(krylov_block), hbm(degree_row))
    row_bits = bits(sources)
    top = row_bits.pop()
    other = swap(scaled, top, 0)
    low = row_bits[:2]
    diag = low[0] | low[1]
    other, share = lax.optimization_barrier((other, share))
    blocks = [(0, scaled), (top, other)]
    for bit in row_bits[:1:-1]:
        stack = swap(jnp.stack([block for _, block in blocks]), bit, 0)
        blocks = blocks + [(at ^ bit, stack[place]) for place, (at, _) in enumerate(blocks)]
    base = [at for at, _ in blocks]
    named = dict(blocks)
    direct = [mask for mask in (low[0], low[1], diag)]
    relayed = [(mask, at) for at in base[1:] for mask in (low[0], low[1], diag) if (mask ^ at) not in direct]
    pieces = [(mask, swap(scaled, mask, 0)) for mask in direct]
    early = blocks + pieces[:2]
    late = pieces[2:] + [(mask ^ at, swap(named[at], mask, 0)) for mask, at in relayed]
    other_share = swap(share, 0, bits(groups)[-1] | 1)
    order = [at for at, _ in early]
    whole = jnp.stack([block for _, block in early])
    far = [block[None] for _, block in late]
    late = [[at] for at, _ in late]
    far[0], other_share = lax.optimization_barrier((far[0], other_share))
    slots = tile_column.shape[2]
    many = groups // 2
    table_shape = (sources * per_piece + 1, vectors, 2 * height)
    index, panel, table = pl.pallas_call(
        lambda *refs: load_kernel(per_piece, sources * per_piece, order, *refs),
        out_shape=[
            pltpu.SMEM((slots, block_rows), jnp.int32),
            jax.ShapeDtypeStruct((block_rows, height, slot_width), BF16),
            jax.ShapeDtypeStruct(table_shape, BF16),
        ],
        in_specs=[pl.BlockSpec(memory_space=pl.ANY)] * 3 + [vmem()],
        out_specs=[smem(), vmem(), vmem()],
        scratch_shapes=[
            pltpu.VMEM((slots, block_rows), jnp.int32),
            pltpu.VMEM((slots, block_rows), jnp.int32),
            pltpu.VMEM((slots, block_rows), jnp.int32),
            pltpu.SemaphoreType.DMA((4,)),
        ],
        compiler_params=limit(2),
        name="load",
    )(hbm(tile_column[:, 0].T), hbm(tile_live[:, 0].T), hbm(tile_values[:, 0]), whole)
    index = pltpu.with_memory_space_constraint(index, pltpu.SMEM)
    lhs = pltpu.VMEM((2, 4 * vectors, slot_width), BF16)
    table, send = pl.pallas_call(
        lambda *refs: send_kernel(groups, per_piece, late, *refs),
        out_shape=[
            jax.ShapeDtypeStruct(table_shape, BF16),
            jax.ShapeDtypeStruct((many, vectors, owned), BF16),
        ],
        in_specs=[smem()] + [vmem()] * (2 + len(far)),
        out_specs=[vmem(), vmem()],
        scratch_shapes=[lhs],
        input_output_aliases={2: 0},
        compiler_params=limit(8),
        name="send",
    )(index, panel, table, *far)
    keep = pl.pallas_call(
        lambda *refs: keep_kernel(groups, per_piece, *refs),
        out_shape=jax.ShapeDtypeStruct((many, vectors, owned), F32),
        in_specs=[smem(), vmem(), vmem()],
        out_specs=vmem(),
        scratch_shapes=[lhs],
        compiler_params=limit(8),
        name="keep",
    )(index, panel, table)
    col_bits = bits(groups)
    last = col_bits.pop()
    for bit in col_bits:
        summed = keep + swap(send, 0, bit | 1).astype(F32)
        if bit != col_bits[-1]:
            pairs = summed.reshape((-1, 2) + summed.shape[1:])
            keep, send = pairs[:, 0], pairs[:, 1].astype(BF16)
    sums = summed.astype(BF16)
    got = swap(sums, 0, last | 1)
    pieces, gram = pl.pallas_call(
        lambda *refs: gram_kernel(last, *refs),
        out_shape=[
            jax.ShapeDtypeStruct((3 * vectors, owned), BF16),
            jax.ShapeDtypeStruct((vectors, 2 * vectors), F32),
        ],
        in_specs=[vmem()] * 4,
        out_specs=[vmem(), vmem()],
        scratch_shapes=[pltpu.VMEM((2, 4 * vectors, owned), BF16)],
        compiler_params=limit(4),
        name="gram",
    )(share, other_share, sums, got)
    for bit in col_bits:
        gram = gram + swap(gram, 0, bit | 1)
    for bit in bits(sources):
        gram = gram + swap(gram, bit, 1)
    total_rows = sources * groups * owned
    orthonormal, quotient = pl.pallas_call(
        lambda *refs: finish_kernel(total_rows, *refs),
        out_shape=[
            jax.ShapeDtypeStruct((vectors, owned), F32),
            jax.ShapeDtypeStruct((vectors, vectors), F32),
        ],
        in_specs=[vmem(), vmem()],
        out_specs=[vmem(), vmem()],
        compiler_params=limit(4),
        name="finish",
    )(gram, pieces)
    return (orthonormal, quotient)


def solution(mesh):
    return jax.shard_map(
        on_device,
        mesh=mesh,
        in_specs=(
            P(None, ("row", "col")),
            P(("row", "col")),
            P("row", "col", None, None),
            P("row", "col", None),
            P("row", "col", None),
        ),
        out_specs=(P(None, ("row", "col")), P()),
        check_vma=False,
    )
```

```python
import math

import jax
import jax.numpy as jnp
from jax import lax
from jax.experimental import pallas as pl
from jax.experimental.pallas import tpu as pltpu
from jax.sharding import PartitionSpec as P

F32 = jnp.float32
BF16 = jnp.bfloat16


def limit(mib):
    return pltpu.CompilerParams(vmem_limit_bytes=mib << 20)


def hbm(value):
    return pltpu.with_memory_space_constraint(value, pltpu.HBM)


def vmem():
    return pl.BlockSpec(memory_space=pltpu.VMEM)


def smem():
    return pl.BlockSpec(memory_space=pltpu.SMEM)


def swap(value, row_mask, col_mask):
    rows, cols = lax.axis_size("row"), lax.axis_size("col")
    pairs = [(r * cols + c, (r ^ row_mask) * cols + (c ^ col_mask)) for r in range(rows) for c in range(cols)]
    return lax.ppermute(value, ("row", "col"), pairs)


def bits(size):
    out = []
    mask = 1
    while mask < size:
        out.append(mask)
        mask *= 2
    return out


def split3(value):
    high = value.astype(BF16)
    rest = value - high.astype(F32)
    mid = rest.astype(BF16)
    low = (rest - mid.astype(F32)).astype(BF16)
    return high, mid, low


def scale_kernel(basis_ref, degree_ref, scaled_ref, share_ref):
    vectors, owned = basis_ref.shape
    basis = basis_ref[...]
    degree = degree_ref[...].astype(F32)
    scaled_ref[...] = (basis.astype(F32) * lax.rsqrt(degree)).astype(BF16)
    share_ref[:vectors, :] = basis
    share_ref[vectors:, :] = jnp.broadcast_to(degree, (16, owned)).astype(BF16)


def fill_table(table_ref, per_piece, height, sources, tiles_of):
    wide = 2 * height
    for source, ref in zip(sources, tiles_of):
        for pair in range(per_piece // 2):
            tile = ref[:, pair * wide:(pair + 1) * wide]
            block = source * per_piece + 2 * pair
            table_ref[block] = tile
            table_ref[block + 1] = jnp.concatenate([tile[:, height:], tile[:, :height]], axis=1)


def load_kernel(per_piece, zero_at, order, column_in, live_in, panel_in, near_ref, index_ref, panel_ref,
                table_ref, column_ref, live_ref, work_ref, sem):
    copies = [
        pltpu.make_async_copy(column_in, column_ref, sem.at[0]),
        pltpu.make_async_copy(live_in, live_ref, sem.at[1]),
        pltpu.make_async_copy(panel_in, panel_ref, sem.at[2]),
    ]
    for copy in copies:
        copy.start()
    fill_table(table_ref, per_piece, panel_ref.shape[1], order, [near_ref.at[at] for at in range(len(order))])
    table_ref[zero_at] = jnp.zeros(table_ref.shape[1:], BF16)
    copies[0].wait()
    copies[1].wait()
    column = column_ref[...] ^ (lax.axis_index("row") * per_piece)
    slot = lax.broadcasted_iota(jnp.int32, column.shape, 0)
    column = column ^ (slot & 1)
    work_ref[...] = jnp.where(live_ref[...] == 1, column, zero_at)
    last = pltpu.make_async_copy(work_ref, index_ref, sem.at[3])
    last.start()
    copies[2].wait()
    last.wait()


def multiply(groups, per_piece, odd, index_ref, panel_ref, table_ref, lhs_ref, out_ref):
    height = panel_ref.shape[1]
    slots = index_ref.shape[0]
    vectors = table_ref.shape[1]
    wide = 2 * height
    my_col = lax.axis_index("col")
    is_low = lax.broadcasted_iota(jnp.int32, (vectors, wide), 1) < height
    pack = 4
    span = pack * height

    def chunk_of(step, chunk):
        flips = odd
        for bit in bits(groups)[:-1]:
            flips = flips ^ ((step // bit) & 1)
        row0 = ((2 * step + flips) ^ my_col) * per_piece + chunk * pack
        slot_of = chunk % 2
        for inner in range(pack):
            row = row0 + inner
            for pair in range(slots // 2):
                first = index_ref[2 * pair, row]
                second = index_ref[2 * pair + 1, row]
                lhs_ref[slot_of, inner * vectors:(inner + 1) * vectors, pair * wide:(pair + 1) * wide] = jnp.where(
                    is_low, table_ref[first], table_ref[second])
        rhs = panel_ref[pl.ds(row0, pack)].reshape(pack * height, slots * height)
        prod = lax.dot_general(lhs_ref[slot_of], rhs, (((1,), (1,)), ((), ())), preferred_element_type=F32)
        for pair in range(pack // 2):
            lanes = slice(pair * wide, (pair + 1) * wide)
            top = prod[2 * pair * vectors:(2 * pair + 1) * vectors, lanes]
            low = prod[(2 * pair + 1) * vectors:(2 * pair + 2) * vectors, lanes]
            at = chunk * span + pair * wide
            out_ref[step, :, at:at + wide] = jnp.where(is_low, top, low).astype(out_ref.dtype)

    if groups <= 4:
        for step in range(groups // 2):
            for chunk in range(per_piece // pack):
                chunk_of(step, chunk)
    else:
        def body(step, carry):
            for chunk in range(per_piece // pack):
                chunk_of(step, chunk)
            return carry

        lax.fori_loop(0, groups // 2, body, 0)


def send_kernel(groups, per_piece, orders, index_ref, panel_ref, table_in, *refs):
    table_ref, send_ref, lhs_ref = refs[len(orders):]
    for order, ref in zip(orders, refs):
        fill_table(table_ref, per_piece, panel_ref.shape[1], order, [ref.at[at] for at in range(len(order))])
    multiply(groups, per_piece, 1, index_ref, panel_ref, table_ref, lhs_ref, send_ref)


def keep_kernel(groups, per_piece, index_ref, panel_ref, table_ref, keep_ref, lhs_ref):
    multiply(groups, per_piece, 0, index_ref, panel_ref, table_ref, lhs_ref, keep_ref)


def gram_kernel(last, mine_ref, theirs_ref, sums_ref, got_ref, split_ref, gram_ref, stack_ref):
    vectors = mine_ref.shape[0] - 16
    upper = (lax.axis_index("col") // last) & 1
    for place, share_ref in ((0, mine_ref), (1, theirs_ref)):
        basis = share_ref[:vectors, :]
        inv_root = lax.rsqrt(share_ref[vectors:, :].astype(F32))[:1]
        spread = sums_ref[place].astype(F32) + got_ref[1 - place].astype(F32)
        applied = basis.astype(F32) - inv_root * spread
        slot = upper if place == 0 else 1 - upper
        for at, piece in enumerate(split3(applied)):
            if place == 0:
                split_ref[at * vectors:(at + 1) * vectors, :] = piece
            stack_ref[slot, at * vectors:(at + 1) * vectors, :] = piece
        stack_ref[slot, 3 * vectors:4 * vectors, :] = basis
    dims = (((1,), (1,)), ((), ()))
    first, second = stack_ref[0], stack_ref[1]
    prod = lax.dot_general(first, first, dims, preferred_element_type=F32) + lax.dot_general(
        second, second, dims, preferred_element_type=F32)
    wide = 2 * vectors
    near = prod[:, :wide]
    far = prod[:, wide:]

    def rows(value, at):
        return value[at * vectors:(at + 1) * vectors]

    energy_low = rows(near, 0) + (rows(near, 1) + (rows(near, 2) + rows(far, 0)))
    energy_high = rows(near, 0) + rows(near, 1)
    quotient_low = rows(near, 3) + rows(far, 3)
    quotient_high = rows(near, 3)
    lane = lax.broadcasted_iota(jnp.int32, (vectors, wide), 1)
    gram_ref[...] = jnp.where(
        lane < vectors,
        energy_low + pltpu.roll(energy_high, vectors, 1),
        quotient_high + pltpu.roll(quotient_low, vectors, 1),
    )


def finish_kernel(total_rows, gram_ref, split_ref, out_ref, quotient_ref):
    vectors = gram_ref.shape[0]
    wide = 2 * vectors
    gram = gram_ref[...]
    quotient_ref[...] = (gram / total_rows)[:, vectors:]
    row = lax.broadcasted_iota(jnp.int32, (vectors, wide), 0)
    lane = lax.broadcasted_iota(jnp.int32, (vectors, wide), 1)
    work = jnp.where(lane < vectors, gram, jnp.where(lane == row + vectors, 1.0, 0.0))
    height = 8
    tiles = [work[at * height:(at + 1) * height] for at in range(vectors // height)]
    below = lax.broadcasted_iota(jnp.int32, (height, wide), 0)

    def across(tile, at):
        return jnp.broadcast_to(tile[:, at:at + 1], (height, wide))

    def down(tile, at):
        return jnp.broadcast_to(tile[at:at + 1], (height, wide))

    for home in range(len(tiles)):
        columns = [[across(tile, home * height + at) for at in range(height)] for tile in tiles[home:]]
        for at in range(height):
            own = columns[0]
            scale = 1.0 / down(own[at], at)
            pivot_row = down(tiles[home], at)
            entries = [down(own[later], at) for later in range(height)]
            for place, column in enumerate(columns):
                lower = jnp.where(below > at, column[at], 0.0) if place == 0 else column[at]
                factor = lower * scale
                tiles[home + place] = tiles[home + place] - factor * pivot_row
                for later in range(at + 1, height):
                    if place == 0 and later == at + 1:
                        column[later] = column[later] - (lower * entries[later]) * scale
                    else:
                        column[later] = column[later] - factor * entries[later]
    done = jnp.concatenate(tiles, axis=0)
    pivot = jnp.sum(jnp.where(lane == row, done, 0.0), axis=1, keepdims=True)
    inverse = done * (lax.rsqrt(pivot) * math.sqrt(total_rows))
    inverse = inverse[:, vectors:]
    w_high, w_mid, w_low = split3(inverse)
    left = jnp.concatenate([w_high, w_high, w_high, w_mid, w_mid, w_low], axis=1)
    pieces = split_ref[...]
    right = jnp.concatenate([pieces, pieces[:2 * vectors], pieces[:vectors]], axis=0)
    out_ref[...] = jnp.dot(left, right, preferred_element_type=F32)


def on_device(krylov_block, degree, tile_values, tile_column, tile_live):
    vectors, owned = krylov_block.shape
    block_rows, _, height, slot_width = tile_values.shape
    sources = lax.axis_size("row")
    groups = lax.axis_size("col")
    per_piece = owned // height
    degree_row = degree.reshape(1, owned)
    scaled, share = pl.pallas_call(
        scale_kernel,
        out_shape=[
            jax.ShapeDtypeStruct((vectors, owned), BF16),
            jax.ShapeDtypeStruct((vectors + 16, owned), BF16),
        ],
        in_specs=[vmem(), vmem()],
        out_specs=[vmem(), vmem()],
        compiler_params=limit(2),
        name="scale",
    )(hbm(krylov_block), hbm(degree_row))
    row_bits = bits(sources)
    top = row_bits.pop()
    other = swap(scaled, top, 0)
    low = row_bits[:2]
    diag = low[0] | low[1]
    other, share = lax.optimization_barrier((other, share))
    blocks = [(0, scaled), (top, other)]
    for bit in row_bits[:1:-1]:
        stack = swap(jnp.stack([block for _, block in blocks]), bit, 0)
        blocks = blocks + [(at ^ bit, stack[place]) for place, (at, _) in enumerate(blocks)]
    base = [at for at, _ in blocks]
    named = dict(blocks)
    direct = [mask for mask in (low[0], low[1], diag)]
    relayed = [(mask, at) for at in base[1:] for mask in (low[0], low[1], diag) if (mask ^ at) not in direct]
    pieces = [(mask, swap(scaled, mask, 0)) for mask in direct]
    early = blocks + pieces[:2]
    late = pieces[2:] + [(mask ^ at, swap(named[at], mask, 0)) for mask, at in relayed]
    other_share = swap(share, 0, bits(groups)[-1] | 1)
    order = [at for at, _ in early]
    whole = jnp.stack([block for _, block in early])
    far = [block[None] for _, block in late]
    late = [[at] for at, _ in late]
    slots = tile_column.shape[2]
    many = groups // 2
    table_shape = (sources * per_piece + 1, vectors, 2 * height)
    index, panel, table = pl.pallas_call(
        lambda *refs: load_kernel(per_piece, sources * per_piece, order, *refs),
        out_shape=[
            pltpu.SMEM((slots, block_rows), jnp.int32),
            jax.ShapeDtypeStruct((block_rows, height, slot_width), BF16),
            jax.ShapeDtypeStruct(table_shape, BF16),
        ],
        in_specs=[pl.BlockSpec(memory_space=pl.ANY)] * 3 + [vmem()],
        out_specs=[smem(), vmem(), vmem()],
        scratch_shapes=[
            pltpu.VMEM((slots, block_rows), jnp.int32),
            pltpu.VMEM((slots, block_rows), jnp.int32),
            pltpu.VMEM((slots, block_rows), jnp.int32),
            pltpu.SemaphoreType.DMA((4,)),
        ],
        compiler_params=limit(2),
        name="load",
    )(hbm(tile_column[:, 0].T), hbm(tile_live[:, 0].T), hbm(tile_values[:, 0]), whole)
    index = pltpu.with_memory_space_constraint(index, pltpu.SMEM)
    lhs = pltpu.VMEM((2, 4 * vectors, slot_width), BF16)
    table, send = pl.pallas_call(
        lambda *refs: send_kernel(groups, per_piece, late, *refs),
        out_shape=[
            jax.ShapeDtypeStruct(table_shape, BF16),
            jax.ShapeDtypeStruct((many, vectors, owned), BF16),
        ],
        in_specs=[smem()] + [vmem()] * (2 + len(far)),
        out_specs=[vmem(), vmem()],
        scratch_shapes=[lhs],
        input_output_aliases={2: 0},
        compiler_params=limit(8),
        name="send",
    )(index, panel, table, *far)
    send, other_share = lax.optimization_barrier((send, other_share))
    keep = pl.pallas_call(
        lambda *refs: keep_kernel(groups, per_piece, *refs),
        out_shape=jax.ShapeDtypeStruct((many, vectors, owned), F32),
        in_specs=[smem(), vmem(), vmem()],
        out_specs=vmem(),
        scratch_shapes=[lhs],
        compiler_params=limit(8),
        name="keep",
    )(index, panel, table)
    col_bits = bits(groups)
    last = col_bits.pop()
    for bit in col_bits:
        summed = keep + swap(send, 0, bit | 1).astype(F32)
        if bit != col_bits[-1]:
            pairs = summed.reshape((-1, 2) + summed.shape[1:])
            keep, send = pairs[:, 0], pairs[:, 1].astype(BF16)
    sums = summed.astype(BF16)
    got = swap(sums, 0, last | 1)
    pieces, gram = pl.pallas_call(
        lambda *refs: gram_kernel(last, *refs),
        out_shape=[
            jax.ShapeDtypeStruct((3 * vectors, owned), BF16),
            jax.ShapeDtypeStruct((vectors, 2 * vectors), F32),
        ],
        in_specs=[vmem()] * 4,
        out_specs=[vmem(), vmem()],
        scratch_shapes=[pltpu.VMEM((2, 4 * vectors, owned), BF16)],
        compiler_params=limit(4),
        name="gram",
    )(share, other_share, sums, got)
    for bit in col_bits:
        gram = gram + swap(gram, 0, bit | 1)
    row_bits = bits(sources)
    for bit in row_bits[2:]:
        gram = gram + swap(gram, bit, 1)
    near = [swap(gram, mask, 1) for mask in (row_bits[0] | row_bits[1], row_bits[0], row_bits[1])]
    gram = (gram + near[0]) + (near[1] + near[2])
    total_rows = sources * groups * owned
    orthonormal, quotient = pl.pallas_call(
        lambda *refs: finish_kernel(total_rows, *refs),
        out_shape=[
            jax.ShapeDtypeStruct((vectors, owned), F32),
            jax.ShapeDtypeStruct((vectors, vectors), F32),
        ],
        in_specs=[vmem(), vmem()],
        out_specs=[vmem(), vmem()],
        compiler_params=limit(4),
        name="finish",
    )(gram, pieces)
    return (orthonormal, quotient)


def solution(mesh):
    return jax.shard_map(
        on_device,
        mesh=mesh,
        in_specs=(
            P(None, ("row", "col")),
            P(("row", "col")),
            P("row", "col", None, None),
            P("row", "col", None),
            P("row", "col", None),
        ),
        out_specs=(P(None, ("row", "col")), P()),
        check_vma=False,
    )
```

```python
import math

import jax
import jax.numpy as jnp
from jax import lax
from jax.experimental import pallas as pl
from jax.experimental.pallas import tpu as pltpu
from jax.sharding import PartitionSpec as P

F32 = jnp.float32
BF16 = jnp.bfloat16


def limit(mib):
    return pltpu.CompilerParams(vmem_limit_bytes=mib << 20)


def hbm(value):
    return pltpu.with_memory_space_constraint(value, pltpu.HBM)


def vmem():
    return pl.BlockSpec(memory_space=pltpu.VMEM)


def smem():
    return pl.BlockSpec(memory_space=pltpu.SMEM)


def swap(value, row_mask, col_mask):
    rows, cols = lax.axis_size("row"), lax.axis_size("col")
    pairs = [(r * cols + c, (r ^ row_mask) * cols + (c ^ col_mask)) for r in range(rows) for c in range(cols)]
    return lax.ppermute(value, ("row", "col"), pairs)


def bits(size):
    out = []
    mask = 1
    while mask < size:
        out.append(mask)
        mask *= 2
    return out


def split3(value):
    high = value.astype(BF16)
    rest = value - high.astype(F32)
    mid = rest.astype(BF16)
    low = (rest - mid.astype(F32)).astype(BF16)
    return high, mid, low


def scale_kernel(basis_ref, degree_ref, scaled_ref, share_ref):
    vectors, owned = basis_ref.shape
    basis = basis_ref[...]
    degree = degree_ref[...].astype(F32)
    scaled_ref[...] = (basis.astype(F32) * lax.rsqrt(degree)).astype(BF16)
    share_ref[:vectors, :] = basis
    share_ref[vectors:, :] = jnp.broadcast_to(degree, (16, owned)).astype(BF16)


def fill_table(table_ref, per_piece, height, sources, tiles_of):
    wide = 2 * height
    for source, ref in zip(sources, tiles_of):
        for pair in range(per_piece // 2):
            tile = ref[:, pair * wide:(pair + 1) * wide]
            block = source * per_piece + 2 * pair
            table_ref[block] = tile
            table_ref[block + 1] = jnp.concatenate([tile[:, height:], tile[:, :height]], axis=1)


def load_kernel(per_piece, zero_at, order, column_in, live_in, panel_in, near_ref, index_ref, panel_ref,
                table_ref, column_ref, live_ref, work_ref, sem):
    copies = [
        pltpu.make_async_copy(column_in, column_ref, sem.at[0]),
        pltpu.make_async_copy(live_in, live_ref, sem.at[1]),
        pltpu.make_async_copy(panel_in, panel_ref, sem.at[2]),
    ]
    for copy in copies:
        copy.start()
    fill_table(table_ref, per_piece, panel_ref.shape[1], order, [near_ref.at[at] for at in range(len(order))])
    table_ref[zero_at] = jnp.zeros(table_ref.shape[1:], BF16)
    copies[0].wait()
    copies[1].wait()
    column = column_ref[...] ^ (lax.axis_index("row") * per_piece)
    slot = lax.broadcasted_iota(jnp.int32, column.shape, 0)
    column = column ^ (slot & 1)
    work_ref[...] = jnp.where(live_ref[...] == 1, column, zero_at)
    last = pltpu.make_async_copy(work_ref, index_ref, sem.at[3])
    last.start()
    copies[2].wait()
    last.wait()


def multiply(groups, per_piece, odd, index_ref, panel_ref, table_ref, lhs_ref, out_ref):
    height = panel_ref.shape[1]
    slots = index_ref.shape[0]
    vectors = table_ref.shape[1]
    wide = 2 * height
    my_col = lax.axis_index("col")
    is_low = lax.broadcasted_iota(jnp.int32, (vectors, wide), 1) < height
    pack = 4
    span = pack * height

    def chunk_of(step, chunk):
        flips = odd
        for bit in bits(groups)[:-1]:
            flips = flips ^ ((step // bit) & 1)
        row0 = ((2 * step + flips) ^ my_col) * per_piece + chunk * pack
        slot_of = chunk % 2
        for inner in range(pack):
            row = row0 + inner
            for pair in range(slots // 2):
                first = index_ref[2 * pair, row]
                second = index_ref[2 * pair + 1, row]
                lhs_ref[slot_of, inner * vectors:(inner + 1) * vectors, pair * wide:(pair + 1) * wide] = jnp.where(
                    is_low, table_ref[first], table_ref[second])
        rhs = panel_ref[pl.ds(row0, pack)].reshape(pack * height, slots * height)
        prod = lax.dot_general(lhs_ref[slot_of], rhs, (((1,), (1,)), ((), ())), preferred_element_type=F32)
        for pair in range(pack // 2):
            lanes = slice(pair * wide, (pair + 1) * wide)
            top = prod[2 * pair * vectors:(2 * pair + 1) * vectors, lanes]
            low = prod[(2 * pair + 1) * vectors:(2 * pair + 2) * vectors, lanes]
            at = chunk * span + pair * wide
            out_ref[step, :, at:at + wide] = jnp.where(is_low, top, low).astype(out_ref.dtype)

    if groups <= 4:
        for step in range(groups // 2):
            for chunk in range(per_piece // pack):
                chunk_of(step, chunk)
    else:
        def body(step, carry):
            for chunk in range(per_piece // pack):
                chunk_of(step, chunk)
            return carry

        lax.fori_loop(0, groups // 2, body, 0)


def send_kernel(groups, per_piece, orders, index_ref, panel_ref, table_in, *refs):
    table_ref, send_ref, lhs_ref = refs[len(orders):]
    for order, ref in zip(orders, refs):
        fill_table(table_ref, per_piece, panel_ref.shape[1], order, [ref.at[at] for at in range(len(order))])
    multiply(groups, per_piece, 1, index_ref, panel_ref, table_ref, lhs_ref, send_ref)


def keep_kernel(groups, per_piece, index_ref, panel_ref, table_ref, keep_ref, lhs_ref):
    multiply(groups, per_piece, 0, index_ref, panel_ref, table_ref, lhs_ref, keep_ref)


def gram_kernel(last, mine_ref, theirs_ref, sums_ref, got_ref, split_ref, gram_ref, stack_ref):
    vectors = mine_ref.shape[0] - 16
    upper = (lax.axis_index("col") // last) & 1
    for place, share_ref in ((0, mine_ref), (1, theirs_ref)):
        basis = share_ref[:vectors, :]
        inv_root = lax.rsqrt(share_ref[vectors:, :].astype(F32))[:1]
        spread = sums_ref[place].astype(F32) + got_ref[1 - place].astype(F32)
        applied = basis.astype(F32) - inv_root * spread
        slot = upper if place == 0 else 1 - upper
        for at, piece in enumerate(split3(applied)):
            if place == 0:
                split_ref[at * vectors:(at + 1) * vectors, :] = piece
            stack_ref[slot, at * vectors:(at + 1) * vectors, :] = piece
        stack_ref[slot, 3 * vectors:4 * vectors, :] = basis
    dims = (((1,), (1,)), ((), ()))
    first, second = stack_ref[0], stack_ref[1]
    prod = lax.dot_general(first, first, dims, preferred_element_type=F32) + lax.dot_general(
        second, second, dims, preferred_element_type=F32)
    wide = 2 * vectors
    near = prod[:, :wide]
    far = prod[:, wide:]

    def rows(value, at):
        return value[at * vectors:(at + 1) * vectors]

    energy_low = rows(near, 0) + (rows(near, 1) + (rows(near, 2) + rows(far, 0)))
    energy_high = rows(near, 0) + rows(near, 1)
    quotient_low = rows(near, 3) + rows(far, 3)
    quotient_high = rows(near, 3)
    lane = lax.broadcasted_iota(jnp.int32, (vectors, wide), 1)
    gram_ref[...] = jnp.where(
        lane < vectors,
        energy_low + pltpu.roll(energy_high, vectors, 1),
        quotient_high + pltpu.roll(quotient_low, vectors, 1),
    )


def finish_kernel(total_rows, gram_ref, split_ref, out_ref, quotient_ref):
    vectors = gram_ref.shape[0]
    wide = 2 * vectors
    gram = gram_ref[...]
    quotient_ref[...] = (gram / total_rows)[:, vectors:]
    row = lax.broadcasted_iota(jnp.int32, (vectors, wide), 0)
    lane = lax.broadcasted_iota(jnp.int32, (vectors, wide), 1)
    work = jnp.where(lane < vectors, gram, jnp.where(lane == row + vectors, 1.0, 0.0))
    height = 8
    tiles = [work[at * height:(at + 1) * height] for at in range(vectors // height)]
    below = lax.broadcasted_iota(jnp.int32, (height, wide), 0)

    def across(tile, at):
        return jnp.broadcast_to(tile[:, at:at + 1], (height, wide))

    def down(tile, at):
        return jnp.broadcast_to(tile[at:at + 1], (height, wide))

    for home in range(len(tiles)):
        columns = [[across(tile, home * height + at) for at in range(height)] for tile in tiles[home:]]
        for at in range(height):
            own = columns[0]
            scale = 1.0 / down(own[at], at)
            pivot_row = down(tiles[home], at)
            entries = [down(own[later], at) for later in range(height)]
            for place, column in enumerate(columns):
                lower = jnp.where(below > at, column[at], 0.0) if place == 0 else column[at]
                factor = lower * scale
                tiles[home + place] = tiles[home + place] - factor * pivot_row
                for later in range(at + 1, height):
                    if place == 0 and later == at + 1:
                        column[later] = column[later] - (lower * entries[later]) * scale
                    else:
                        column[later] = column[later] - factor * entries[later]
    done = jnp.concatenate(tiles, axis=0)
    pivot = jnp.sum(jnp.where(lane == row, done, 0.0), axis=1, keepdims=True)
    inverse = done * (lax.rsqrt(pivot) * math.sqrt(total_rows))
    inverse = inverse[:, vectors:]
    w_high, w_mid, w_low = split3(inverse)
    left = jnp.concatenate([w_high, w_high, w_high, w_mid, w_mid, w_low], axis=1)
    pieces = split_ref[...]
    right = jnp.concatenate([pieces, pieces[:2 * vectors], pieces[:vectors]], axis=0)
    out_ref[...] = jnp.dot(left, right, preferred_element_type=F32)


def on_device(krylov_block, degree, tile_values, tile_column, tile_live):
    vectors, owned = krylov_block.shape
    block_rows, _, height, slot_width = tile_values.shape
    sources = lax.axis_size("row")
    groups = lax.axis_size("col")
    per_piece = owned // height
    degree_row = degree.reshape(1, owned)
    scaled, share = pl.pallas_call(
        scale_kernel,
        out_shape=[
            jax.ShapeDtypeStruct((vectors, owned), BF16),
            jax.ShapeDtypeStruct((vectors + 16, owned), BF16),
        ],
        in_specs=[vmem(), vmem()],
        out_specs=[vmem(), vmem()],
        compiler_params=limit(2),
        name="scale",
    )(hbm(krylov_block), hbm(degree_row))
    row_bits = bits(sources)
    top = row_bits.pop()
    other = swap(scaled, top, 0)
    low = row_bits[:2]
    diag = low[0] | low[1]
    other, share = lax.optimization_barrier((other, share))
    blocks = [(0, scaled), (top, other)]
    for bit in row_bits[:1:-1]:
        stack = swap(jnp.stack([block for _, block in blocks]), bit, 0)
        blocks = blocks + [(at ^ bit, stack[place]) for place, (at, _) in enumerate(blocks)]
    base = [at for at, _ in blocks]
    named = dict(blocks)
    direct = [mask for mask in (low[0], low[1], diag)]
    relayed = [(mask, at) for at in base[1:] for mask in (diag, low[1], low[0]) if (mask ^ at) not in direct]
    pieces = [(mask, swap(scaled, mask, 0)) for mask in direct]
    early = blocks + pieces[:2]
    late = pieces[2:] + [(mask ^ at, swap(named[at], mask, 0)) for mask, at in relayed]
    other_share = swap(share, 0, bits(groups)[-1] | 1)
    order = [at for at, _ in early]
    whole = jnp.stack([block for _, block in early])
    far = [block[None] for _, block in late]
    late = [[at] for at, _ in late]
    slots = tile_column.shape[2]
    many = groups // 2
    table_shape = (sources * per_piece + 1, vectors, 2 * height)
    index, panel, table = pl.pallas_call(
        lambda *refs: load_kernel(per_piece, sources * per_piece, order, *refs),
        out_shape=[
            pltpu.SMEM((slots, block_rows), jnp.int32),
            jax.ShapeDtypeStruct((block_rows, height, slot_width), BF16),
            jax.ShapeDtypeStruct(table_shape, BF16),
        ],
        in_specs=[pl.BlockSpec(memory_space=pl.ANY)] * 3 + [vmem()],
        out_specs=[smem(), vmem(), vmem()],
        scratch_shapes=[
            pltpu.VMEM((slots, block_rows), jnp.int32),
            pltpu.VMEM((slots, block_rows), jnp.int32),
            pltpu.VMEM((slots, block_rows), jnp.int32),
            pltpu.SemaphoreType.DMA((4,)),
        ],
        compiler_params=limit(2),
        name="load",
    )(hbm(tile_column[:, 0].T), hbm(tile_live[:, 0].T), hbm(tile_values[:, 0]), whole)
    index = pltpu.with_memory_space_constraint(index, pltpu.SMEM)
    lhs = pltpu.VMEM((2, 4 * vectors, slot_width), BF16)
    table, send = pl.pallas_call(
        lambda *refs: send_kernel(groups, per_piece, late, *refs),
        out_shape=[
            jax.ShapeDtypeStruct(table_shape, BF16),
            jax.ShapeDtypeStruct((many, vectors, owned), BF16),
        ],
        in_specs=[smem()] + [vmem()] * (2 + len(far)),
        out_specs=[vmem(), vmem()],
        scratch_shapes=[lhs],
        input_output_aliases={2: 0},
        compiler_params=limit(8),
        name="send",
    )(index, panel, table, *far)
    send, other_share = lax.optimization_barrier((send, other_share))
    keep = pl.pallas_call(
        lambda *refs: keep_kernel(groups, per_piece, *refs),
        out_shape=jax.ShapeDtypeStruct((many, vectors, owned), F32),
        in_specs=[smem(), vmem(), vmem()],
        out_specs=vmem(),
        scratch_shapes=[lhs],
        compiler_params=limit(8),
        name="keep",
    )(index, panel, table)
    col_bits = bits(groups)
    last = col_bits.pop()
    for bit in col_bits:
        summed = keep + swap(send, 0, bit | 1).astype(F32)
        if bit != col_bits[-1]:
            pairs = summed.reshape((-1, 2) + summed.shape[1:])
            keep, send = pairs[:, 0], pairs[:, 1].astype(BF16)
    sums = summed.astype(BF16)
    got = swap(sums, 0, last | 1)
    pieces, gram = pl.pallas_call(
        lambda *refs: gram_kernel(last, *refs),
        out_shape=[
            jax.ShapeDtypeStruct((3 * vectors, owned), BF16),
            jax.ShapeDtypeStruct((vectors, 2 * vectors), F32),
        ],
        in_specs=[vmem()] * 4,
        out_specs=[vmem(), vmem()],
        scratch_shapes=[pltpu.VMEM((2, 4 * vectors, owned), BF16)],
        compiler_params=limit(4),
        name="gram",
    )(share, other_share, sums, got)
    for bit in col_bits:
        gram = gram + swap(gram, 0, bit | 1)
    row_bits = bits(sources)
    for bit in row_bits[2:]:
        gram = gram + swap(gram, bit, 1)
    near = [swap(gram, mask, 1) for mask in (row_bits[0] | row_bits[1], row_bits[0], row_bits[1])]
    gram = (gram + near[0]) + (near[1] + near[2])
    total_rows = sources * groups * owned
    orthonormal, quotient = pl.pallas_call(
        lambda *refs: finish_kernel(total_rows, *refs),
        out_shape=[
            jax.ShapeDtypeStruct((vectors, owned), F32),
            jax.ShapeDtypeStruct((vectors, vectors), F32),
        ],
        in_specs=[vmem(), vmem()],
        out_specs=[vmem(), vmem()],
        compiler_params=limit(4),
        name="finish",
    )(gram, pieces)
    return (orthonormal, quotient)


def solution(mesh):
    return jax.shard_map(
        on_device,
        mesh=mesh,
        in_specs=(
            P(None, ("row", "col")),
            P(("row", "col")),
            P("row", "col", None, None),
            P("row", "col", None),
            P("row", "col", None),
        ),
        out_specs=(P(None, ("row", "col")), P()),
        check_vma=False,
    )
```

```python
import math

import jax
import jax.numpy as jnp
from jax import lax
from jax.experimental import pallas as pl
from jax.experimental.pallas import tpu as pltpu
from jax.sharding import PartitionSpec as P

F32 = jnp.float32
BF16 = jnp.bfloat16


def limit(mib):
    return pltpu.CompilerParams(vmem_limit_bytes=mib << 20)


def hbm(value):
    return pltpu.with_memory_space_constraint(value, pltpu.HBM)


def vmem():
    return pl.BlockSpec(memory_space=pltpu.VMEM)


def smem():
    return pl.BlockSpec(memory_space=pltpu.SMEM)


def swap(value, row_mask, col_mask):
    rows, cols = lax.axis_size("row"), lax.axis_size("col")
    pairs = [(r * cols + c, (r ^ row_mask) * cols + (c ^ col_mask)) for r in range(rows) for c in range(cols)]
    return lax.ppermute(value, ("row", "col"), pairs)


def bits(size):
    out = []
    mask = 1
    while mask < size:
        out.append(mask)
        mask *= 2
    return out


def split3(value):
    high = value.astype(BF16)
    rest = value - high.astype(F32)
    mid = rest.astype(BF16)
    low = (rest - mid.astype(F32)).astype(BF16)
    return high, mid, low


def scale_kernel(basis_ref, degree_ref, scaled_ref, share_ref):
    vectors, owned = basis_ref.shape
    basis = basis_ref[...]
    degree = degree_ref[...].astype(F32)
    scaled_ref[...] = (basis.astype(F32) * lax.rsqrt(degree)).astype(BF16)
    share_ref[:vectors, :] = basis
    share_ref[vectors:, :] = jnp.broadcast_to(degree, (16, owned)).astype(BF16)


def fill_table(table_ref, per_piece, height, sources, tiles_of):
    wide = 2 * height
    for source, ref in zip(sources, tiles_of):
        for pair in range(per_piece // 2):
            tile = ref[:, pair * wide:(pair + 1) * wide]
            block = source * per_piece + 2 * pair
            table_ref[block] = tile
            table_ref[block + 1] = jnp.concatenate([tile[:, height:], tile[:, :height]], axis=1)


def load_kernel(per_piece, zero_at, order, column_in, live_in, panel_in, near_ref, index_ref, panel_ref,
                table_ref, column_ref, live_ref, work_ref, sem):
    copies = [
        pltpu.make_async_copy(column_in, column_ref, sem.at[0]),
        pltpu.make_async_copy(live_in, live_ref, sem.at[1]),
        pltpu.make_async_copy(panel_in, panel_ref, sem.at[2]),
    ]
    for copy in copies:
        copy.start()
    fill_table(table_ref, per_piece, panel_ref.shape[1], order, [near_ref.at[at] for at in range(len(order))])
    table_ref[zero_at] = jnp.zeros(table_ref.shape[1:], BF16)
    copies[0].wait()
    copies[1].wait()
    column = column_ref[...] ^ (lax.axis_index("row") * per_piece)
    slot = lax.broadcasted_iota(jnp.int32, column.shape, 0)
    column = column ^ (slot & 1)
    work_ref[...] = jnp.where(live_ref[...] == 1, column, zero_at)
    last = pltpu.make_async_copy(work_ref, index_ref, sem.at[3])
    last.start()
    copies[2].wait()
    last.wait()


def multiply(groups, per_piece, odd, base, index_ref, panel_ref, table_ref, lhs_ref, out_ref):
    count = out_ref.shape[0]
    height = panel_ref.shape[1]
    slots = index_ref.shape[0]
    vectors = table_ref.shape[1]
    wide = 2 * height
    my_col = lax.axis_index("col")
    is_low = lax.broadcasted_iota(jnp.int32, (vectors, wide), 1) < height
    pack = 4
    span = pack * height

    def chunk_of(step, chunk):
        flips = odd
        for bit in bits(groups)[:-1]:
            flips = flips ^ (((base + step) // bit) & 1)
        row0 = ((2 * (base + step) + flips) ^ my_col) * per_piece + chunk * pack
        slot_of = chunk % 2
        for inner in range(pack):
            row = row0 + inner
            for pair in range(slots // 2):
                first = index_ref[2 * pair, row]
                second = index_ref[2 * pair + 1, row]
                lhs_ref[slot_of, inner * vectors:(inner + 1) * vectors, pair * wide:(pair + 1) * wide] = jnp.where(
                    is_low, table_ref[first], table_ref[second])
        rhs = panel_ref[pl.ds(row0, pack)].reshape(pack * height, slots * height)
        prod = lax.dot_general(lhs_ref[slot_of], rhs, (((1,), (1,)), ((), ())), preferred_element_type=F32)
        for pair in range(pack // 2):
            lanes = slice(pair * wide, (pair + 1) * wide)
            top = prod[2 * pair * vectors:(2 * pair + 1) * vectors, lanes]
            low = prod[(2 * pair + 1) * vectors:(2 * pair + 2) * vectors, lanes]
            at = chunk * span + pair * wide
            out_ref[step, :, at:at + wide] = jnp.where(is_low, top, low).astype(out_ref.dtype)

    if groups <= 4:
        for step in range(count):
            for chunk in range(per_piece // pack):
                chunk_of(step, chunk)
    else:
        def body(step, carry):
            for chunk in range(per_piece // pack):
                chunk_of(step, chunk)
            return carry

        lax.fori_loop(0, count, body, 0)


def send_kernel(groups, per_piece, orders, index_ref, panel_ref, table_in, *refs):
    table_ref, send_ref, lhs_ref = refs[len(orders):]
    for order, ref in zip(orders, refs):
        fill_table(table_ref, per_piece, panel_ref.shape[1], order, [ref.at[at] for at in range(len(order))])
    multiply(groups, per_piece, 1, 0, index_ref, panel_ref, table_ref, lhs_ref, send_ref)


def keep_kernel(groups, per_piece, odd, base, index_ref, panel_ref, table_ref, keep_ref, lhs_ref):
    multiply(groups, per_piece, odd, base, index_ref, panel_ref, table_ref, lhs_ref, keep_ref)


def gram_kernel(last, mine_ref, theirs_ref, sums_ref, got_ref, split_ref, gram_ref, stack_ref):
    vectors = mine_ref.shape[0] - 16
    upper = (lax.axis_index("col") // last) & 1
    for place, share_ref in ((0, mine_ref), (1, theirs_ref)):
        basis = share_ref[:vectors, :]
        inv_root = lax.rsqrt(share_ref[vectors:, :].astype(F32))[:1]
        spread = sums_ref[place].astype(F32) + got_ref[1 - place].astype(F32)
        applied = basis.astype(F32) - inv_root * spread
        slot = upper if place == 0 else 1 - upper
        for at, piece in enumerate(split3(applied)):
            if place == 0:
                split_ref[at * vectors:(at + 1) * vectors, :] = piece
            stack_ref[slot, at * vectors:(at + 1) * vectors, :] = piece
        stack_ref[slot, 3 * vectors:4 * vectors, :] = basis
    dims = (((1,), (1,)), ((), ()))
    first, second = stack_ref[0], stack_ref[1]
    prod = lax.dot_general(first, first, dims, preferred_element_type=F32) + lax.dot_general(
        second, second, dims, preferred_element_type=F32)
    wide = 2 * vectors
    near = prod[:, :wide]
    far = prod[:, wide:]

    def rows(value, at):
        return value[at * vectors:(at + 1) * vectors]

    energy_low = rows(near, 0) + (rows(near, 1) + (rows(near, 2) + rows(far, 0)))
    energy_high = rows(near, 0) + rows(near, 1)
    quotient_low = rows(near, 3) + rows(far, 3)
    quotient_high = rows(near, 3)
    lane = lax.broadcasted_iota(jnp.int32, (vectors, wide), 1)
    gram_ref[...] = jnp.where(
        lane < vectors,
        energy_low + pltpu.roll(energy_high, vectors, 1),
        quotient_high + pltpu.roll(quotient_low, vectors, 1),
    )


def finish_kernel(total_rows, gram_ref, split_ref, out_ref, quotient_ref):
    vectors = gram_ref.shape[0]
    wide = 2 * vectors
    gram = gram_ref[...]
    quotient_ref[...] = (gram / total_rows)[:, vectors:]
    row = lax.broadcasted_iota(jnp.int32, (vectors, wide), 0)
    lane = lax.broadcasted_iota(jnp.int32, (vectors, wide), 1)
    work = jnp.where(lane < vectors, gram, jnp.where(lane == row + vectors, 1.0, 0.0))
    height = 8
    tiles = [work[at * height:(at + 1) * height] for at in range(vectors // height)]
    below = lax.broadcasted_iota(jnp.int32, (height, wide), 0)

    def across(tile, at):
        return jnp.broadcast_to(tile[:, at:at + 1], (height, wide))

    def down(tile, at):
        return jnp.broadcast_to(tile[at:at + 1], (height, wide))

    for home in range(len(tiles)):
        columns = [[across(tile, home * height + at) for at in range(height)] for tile in tiles[home:]]
        for at in range(height):
            own = columns[0]
            scale = 1.0 / down(own[at], at)
            pivot_row = down(tiles[home], at)
            entries = [down(own[later], at) for later in range(height)]
            for place, column in enumerate(columns):
                lower = jnp.where(below > at, column[at], 0.0) if place == 0 else column[at]
                factor = lower * scale
                tiles[home + place] = tiles[home + place] - factor * pivot_row
                for later in range(at + 1, height):
                    if place == 0 and later == at + 1:
                        column[later] = column[later] - (lower * entries[later]) * scale
                    else:
                        column[later] = column[later] - factor * entries[later]
    done = jnp.concatenate(tiles, axis=0)
    pivot = jnp.sum(jnp.where(lane == row, done, 0.0), axis=1, keepdims=True)
    inverse = done * (lax.rsqrt(pivot) * math.sqrt(total_rows))
    inverse = inverse[:, vectors:]
    w_high, w_mid, w_low = split3(inverse)
    left = jnp.concatenate([w_high, w_high, w_high, w_mid, w_mid, w_low], axis=1)
    pieces = split_ref[...]
    right = jnp.concatenate([pieces, pieces[:2 * vectors], pieces[:vectors]], axis=0)
    out_ref[...] = jnp.dot(left, right, preferred_element_type=F32)


def on_device(krylov_block, degree, tile_values, tile_column, tile_live):
    vectors, owned = krylov_block.shape
    block_rows, _, height, slot_width = tile_values.shape
    sources = lax.axis_size("row")
    groups = lax.axis_size("col")
    per_piece = owned // height
    degree_row = degree.reshape(1, owned)
    scaled, share = pl.pallas_call(
        scale_kernel,
        out_shape=[
            jax.ShapeDtypeStruct((vectors, owned), BF16),
            jax.ShapeDtypeStruct((vectors + 16, owned), BF16),
        ],
        in_specs=[vmem(), vmem()],
        out_specs=[vmem(), vmem()],
        compiler_params=limit(2),
        name="scale",
    )(hbm(krylov_block), hbm(degree_row))
    row_bits = bits(sources)
    top = row_bits.pop()
    other = swap(scaled, top, 0)
    low = row_bits[:2]
    diag = low[0] | low[1]
    other, share = lax.optimization_barrier((other, share))
    blocks = [(0, scaled), (top, other)]
    for bit in row_bits[:1:-1]:
        stack = swap(jnp.stack([block for _, block in blocks]), bit, 0)
        blocks = blocks + [(at ^ bit, stack[place]) for place, (at, _) in enumerate(blocks)]
    base = [at for at, _ in blocks]
    named = dict(blocks)
    direct = [mask for mask in (low[0], low[1], diag)]
    relayed = [(mask, at) for at in base[1:] for mask in (diag, low[1], low[0]) if (mask ^ at) not in direct]
    pieces = [(mask, swap(scaled, mask, 0)) for mask in direct]
    early = blocks + pieces[:2]
    late = pieces[2:] + [(mask ^ at, swap(named[at], mask, 0)) for mask, at in relayed]
    other_share = swap(share, 0, bits(groups)[-1] | 1)
    order = [at for at, _ in early]
    whole = jnp.stack([block for _, block in early])
    far = [block[None] for _, block in late]
    late = [[at] for at, _ in late]
    slots = tile_column.shape[2]
    many = groups // 2
    table_shape = (sources * per_piece + 1, vectors, 2 * height)
    index, panel, table = pl.pallas_call(
        lambda *refs: load_kernel(per_piece, sources * per_piece, order, *refs),
        out_shape=[
            pltpu.SMEM((slots, block_rows), jnp.int32),
            jax.ShapeDtypeStruct((block_rows, height, slot_width), BF16),
            jax.ShapeDtypeStruct(table_shape, BF16),
        ],
        in_specs=[pl.BlockSpec(memory_space=pl.ANY)] * 3 + [vmem()],
        out_specs=[smem(), vmem(), vmem()],
        scratch_shapes=[
            pltpu.VMEM((slots, block_rows), jnp.int32),
            pltpu.VMEM((slots, block_rows), jnp.int32),
            pltpu.VMEM((slots, block_rows), jnp.int32),
            pltpu.SemaphoreType.DMA((4,)),
        ],
        compiler_params=limit(2),
        name="load",
    )(hbm(tile_column[:, 0].T), hbm(tile_live[:, 0].T), hbm(tile_values[:, 0]), whole)
    index = pltpu.with_memory_space_constraint(index, pltpu.SMEM)
    lhs = pltpu.VMEM((2, 4 * vectors, slot_width), BF16)
    table, send = pl.pallas_call(
        lambda *refs: send_kernel(groups, per_piece, late, *refs),
        out_shape=[
            jax.ShapeDtypeStruct(table_shape, BF16),
            jax.ShapeDtypeStruct((many // 2, vectors, owned), BF16),
        ],
        in_specs=[smem()] + [vmem()] * (2 + len(far)),
        out_specs=[vmem(), vmem()],
        scratch_shapes=[lhs],
        input_output_aliases={2: 0},
        compiler_params=limit(8),
        name="send",
    )(index, panel, table, *far)
    send, other_share = lax.optimization_barrier((send, other_share))
    more = pl.pallas_call(
        lambda *refs: keep_kernel(groups, per_piece, 1, many // 2, *refs),
        out_shape=jax.ShapeDtypeStruct((many // 2, vectors, owned), BF16),
        in_specs=[smem(), vmem(), vmem()],
        out_specs=vmem(),
        scratch_shapes=[lhs],
        compiler_params=limit(8),
        name="more",
    )(index, panel, table)
    keep = pl.pallas_call(
        lambda *refs: keep_kernel(groups, per_piece, 0, 0, *refs),
        out_shape=jax.ShapeDtypeStruct((many, vectors, owned), F32),
        in_specs=[smem(), vmem(), vmem()],
        out_specs=vmem(),
        scratch_shapes=[lhs],
        compiler_params=limit(8),
        name="keep",
    )(index, panel, table)
    col_bits = bits(groups)
    last = col_bits.pop()
    for bit in col_bits:
        if bit == col_bits[0]:
            got = jnp.concatenate([swap(send, 0, bit | 1), swap(more, 0, bit | 1)], axis=0)
        else:
            got = swap(send, 0, bit | 1)
        summed = keep + got.astype(F32)
        if bit != col_bits[-1]:
            pairs = summed.reshape((-1, 2) + summed.shape[1:])
            keep, send = pairs[:, 0], pairs[:, 1].astype(BF16)
    sums = summed.astype(BF16)
    got = swap(sums, 0, last | 1)
    pieces, gram = pl.pallas_call(
        lambda *refs: gram_kernel(last, *refs),
        out_shape=[
            jax.ShapeDtypeStruct((3 * vectors, owned), BF16),
            jax.ShapeDtypeStruct((vectors, 2 * vectors), F32),
        ],
        in_specs=[vmem()] * 4,
        out_specs=[vmem(), vmem()],
        scratch_shapes=[pltpu.VMEM((2, 4 * vectors, owned), BF16)],
        compiler_params=limit(4),
        name="gram",
    )(share, other_share, sums, got)
    for bit in col_bits:
        gram = gram + swap(gram, 0, bit | 1)
    row_bits = bits(sources)
    for bit in row_bits[2:]:
        gram = gram + swap(gram, bit, 1)
    near = [swap(gram, mask, 1) for mask in (row_bits[0] | row_bits[1], row_bits[0], row_bits[1])]
    gram = (gram + near[0]) + (near[1] + near[2])
    total_rows = sources * groups * owned
    orthonormal, quotient = pl.pallas_call(
        lambda *refs: finish_kernel(total_rows, *refs),
        out_shape=[
            jax.ShapeDtypeStruct((vectors, owned), F32),
            jax.ShapeDtypeStruct((vectors, vectors), F32),
        ],
        in_specs=[vmem(), vmem()],
        out_specs=[vmem(), vmem()],
        compiler_params=limit(4),
        name="finish",
    )(gram, pieces)
    return (orthonormal, quotient)


def solution(mesh):
    return jax.shard_map(
        on_device,
        mesh=mesh,
        in_specs=(
            P(None, ("row", "col")),
            P(("row", "col")),
            P("row", "col", None, None),
            P("row", "col", None),
            P("row", "col", None),
        ),
        out_specs=(P(None, ("row", "col")), P()),
        check_vma=False,
    )
```

```python
import math

import jax
import jax.numpy as jnp
from jax import lax
from jax.experimental import pallas as pl
from jax.experimental.pallas import tpu as pltpu
from jax.sharding import PartitionSpec as P

F32 = jnp.float32
BF16 = jnp.bfloat16


def limit(mib):
    return pltpu.CompilerParams(vmem_limit_bytes=mib << 20)


def hbm(value):
    return pltpu.with_memory_space_constraint(value, pltpu.HBM)


def vmem():
    return pl.BlockSpec(memory_space=pltpu.VMEM)


def smem():
    return pl.BlockSpec(memory_space=pltpu.SMEM)


def swap(value, row_mask, col_mask):
    rows, cols = lax.axis_size("row"), lax.axis_size("col")
    pairs = [(r * cols + c, (r ^ row_mask) * cols + (c ^ col_mask)) for r in range(rows) for c in range(cols)]
    return lax.ppermute(value, ("row", "col"), pairs)


def bits(size):
    out = []
    mask = 1
    while mask < size:
        out.append(mask)
        mask *= 2
    return out


def split3(value):
    high = value.astype(BF16)
    rest = value - high.astype(F32)
    mid = rest.astype(BF16)
    low = (rest - mid.astype(F32)).astype(BF16)
    return high, mid, low


def scale_kernel(basis_ref, degree_ref, scaled_ref, share_ref):
    vectors, owned = basis_ref.shape
    basis = basis_ref[...]
    degree = degree_ref[...].astype(F32)
    scaled_ref[...] = (basis.astype(F32) * lax.rsqrt(degree)).astype(BF16)
    share_ref[:vectors, :] = basis
    share_ref[vectors:, :] = jnp.broadcast_to(degree, (16, owned)).astype(BF16)


def fill_table(table_ref, per_piece, height, sources, tiles_of):
    wide = 2 * height
    for source, ref in zip(sources, tiles_of):
        for pair in range(per_piece // 2):
            tile = ref[:, pair * wide:(pair + 1) * wide]
            block = source * per_piece + 2 * pair
            table_ref[block] = tile
            table_ref[block + 1] = jnp.concatenate([tile[:, height:], tile[:, :height]], axis=1)


def load_kernel(per_piece, zero_at, order, column_in, live_in, panel_in, near_ref, index_ref, panel_ref,
                table_ref, column_ref, live_ref, work_ref, sem):
    copies = [
        pltpu.make_async_copy(column_in, column_ref, sem.at[0]),
        pltpu.make_async_copy(live_in, live_ref, sem.at[1]),
        pltpu.make_async_copy(panel_in, panel_ref, sem.at[2]),
    ]
    for copy in copies:
        copy.start()
    fill_table(table_ref, per_piece, panel_ref.shape[1], order, [near_ref.at[at] for at in range(len(order))])
    table_ref[zero_at] = jnp.zeros(table_ref.shape[1:], BF16)
    copies[0].wait()
    copies[1].wait()
    column = column_ref[...] ^ (lax.axis_index("row") * per_piece)
    slot = lax.broadcasted_iota(jnp.int32, column.shape, 0)
    column = column ^ (slot & 1)
    work_ref[...] = jnp.where(live_ref[...] == 1, column, zero_at)
    last = pltpu.make_async_copy(work_ref, index_ref, sem.at[3])
    last.start()
    copies[2].wait()
    last.wait()


def multiply(groups, per_piece, odd, index_ref, panel_ref, table_ref, lhs_ref, out_ref):
    height = panel_ref.shape[1]
    slots = index_ref.shape[0]
    vectors = table_ref.shape[1]
    wide = 2 * height
    my_col = lax.axis_index("col")
    is_low = lax.broadcasted_iota(jnp.int32, (vectors, wide), 1) < height
    pack = 4
    span = pack * height

    def chunk_of(step, chunk):
        flips = odd
        for bit in bits(groups)[:-1]:
            flips = flips ^ ((step // bit) & 1)
        row0 = ((2 * step + flips) ^ my_col) * per_piece + chunk * pack
        slot_of = chunk % 2
        for inner in range(pack):
            row = row0 + inner
            for pair in range(slots // 2):
                first = index_ref[2 * pair, row]
                second = index_ref[2 * pair + 1, row]
                lhs_ref[slot_of, inner * vectors:(inner + 1) * vectors, pair * wide:(pair + 1) * wide] = jnp.where(
                    is_low, table_ref[first], table_ref[second])
        rhs = panel_ref[pl.ds(row0, pack)].reshape(pack * height, slots * height)
        prod = lax.dot_general(lhs_ref[slot_of], rhs, (((1,), (1,)), ((), ())), preferred_element_type=F32)
        for pair in range(pack // 2):
            lanes = slice(pair * wide, (pair + 1) * wide)
            top = prod[2 * pair * vectors:(2 * pair + 1) * vectors, lanes]
            low = prod[(2 * pair + 1) * vectors:(2 * pair + 2) * vectors, lanes]
            at = chunk * span + pair * wide
            out_ref[step, :, at:at + wide] = jnp.where(is_low, top, low).astype(out_ref.dtype)

    if groups <= 4:
        for step in range(groups // 2):
            for chunk in range(per_piece // pack):
                chunk_of(step, chunk)
    else:
        def body(step, carry):
            for chunk in range(per_piece // pack):
                chunk_of(step, chunk)
            return carry

        lax.fori_loop(0, groups // 2, body, 0)


def send_kernel(groups, per_piece, orders, index_ref, panel_ref, table_in, *refs):
    table_ref, send_ref, lhs_ref = refs[len(orders):]
    for order, ref in zip(orders, refs):
        fill_table(table_ref, per_piece, panel_ref.shape[1], order, [ref.at[at] for at in range(len(order))])
    multiply(groups, per_piece, 1, index_ref, panel_ref, table_ref, lhs_ref, send_ref)


def keep_kernel(groups, per_piece, index_ref, panel_ref, table_ref, keep_ref, lhs_ref):
    multiply(groups, per_piece, 0, index_ref, panel_ref, table_ref, lhs_ref, keep_ref)


def gram_kernel(last, mine_ref, theirs_ref, sums_ref, got_ref, split_ref, gram_ref, stack_ref):
    vectors = mine_ref.shape[0] - 16
    upper = (lax.axis_index("col") // last) & 1
    for place, share_ref in ((0, mine_ref), (1, theirs_ref)):
        basis = share_ref[:vectors, :]
        inv_root = lax.rsqrt(share_ref[vectors:, :].astype(F32))[:1]
        spread = sums_ref[place].astype(F32) + got_ref[1 - place].astype(F32)
        applied = basis.astype(F32) - inv_root * spread
        slot = upper if place == 0 else 1 - upper
        for at, piece in enumerate(split3(applied)):
            if place == 0:
                split_ref[at * vectors:(at + 1) * vectors, :] = piece
            stack_ref[slot, at * vectors:(at + 1) * vectors, :] = piece
        stack_ref[slot, 3 * vectors:4 * vectors, :] = basis
    dims = (((1,), (1,)), ((), ()))
    first, second = stack_ref[0], stack_ref[1]
    prod = lax.dot_general(first, first, dims, preferred_element_type=F32) + lax.dot_general(
        second, second, dims, preferred_element_type=F32)
    wide = 2 * vectors
    near = prod[:, :wide]
    far = prod[:, wide:]

    def rows(value, at):
        return value[at * vectors:(at + 1) * vectors]

    energy_low = rows(near, 0) + (rows(near, 1) + (rows(near, 2) + rows(far, 0)))
    energy_high = rows(near, 0) + rows(near, 1)
    quotient_low = rows(near, 3) + rows(far, 3)
    quotient_high = rows(near, 3)
    lane = lax.broadcasted_iota(jnp.int32, (vectors, wide), 1)
    gram_ref[...] = jnp.where(
        lane < vectors,
        energy_low + pltpu.roll(energy_high, vectors, 1),
        quotient_high + pltpu.roll(quotient_low, vectors, 1),
    )


def finish_kernel(total_rows, gram_ref, split_ref, out_ref, quotient_ref):
    vectors = gram_ref.shape[0]
    wide = 2 * vectors
    gram = gram_ref[...]
    quotient_ref[...] = (gram / total_rows)[:, vectors:]
    row = lax.broadcasted_iota(jnp.int32, (vectors, wide), 0)
    lane = lax.broadcasted_iota(jnp.int32, (vectors, wide), 1)
    work = jnp.where(lane < vectors, gram, jnp.where(lane == row + vectors, 1.0, 0.0))
    height = 8
    tiles = [work[at * height:(at + 1) * height] for at in range(vectors // height)]
    below = lax.broadcasted_iota(jnp.int32, (height, wide), 0)

    def across(tile, at):
        return jnp.broadcast_to(tile[:, at:at + 1], (height, wide))

    def down(tile, at):
        return jnp.broadcast_to(tile[at:at + 1], (height, wide))

    for home in range(len(tiles)):
        columns = [[across(tile, home * height + at) for at in range(height)] for tile in tiles[home:]]
        for at in range(height):
            own = columns[0]
            scale = 1.0 / down(own[at], at)
            pivot_row = down(tiles[home], at)
            entries = [down(own[later], at) for later in range(height)]
            for place, column in enumerate(columns):
                lower = jnp.where(below > at, column[at], 0.0) if place == 0 else column[at]
                factor = lower * scale
                tiles[home + place] = tiles[home + place] - factor * pivot_row
                for later in range(at + 1, height):
                    if place == 0 and later == at + 1:
                        column[later] = column[later] - (lower * entries[later]) * scale
                    else:
                        column[later] = column[later] - factor * entries[later]
    done = jnp.concatenate(tiles, axis=0)
    pivot = jnp.sum(jnp.where(lane == row, done, 0.0), axis=1, keepdims=True)
    inverse = done * (lax.rsqrt(pivot) * math.sqrt(total_rows))
    inverse = inverse[:, vectors:]
    w_high, w_mid, w_low = split3(inverse)
    left = jnp.concatenate([w_high, w_high, w_high, w_mid, w_mid, w_low], axis=1)
    pieces = split_ref[...]
    right = jnp.concatenate([pieces, pieces[:2 * vectors], pieces[:vectors]], axis=0)
    out_ref[...] = jnp.dot(left, right, preferred_element_type=F32)


def on_device(krylov_block, degree, tile_values, tile_column, tile_live):
    vectors, owned = krylov_block.shape
    block_rows, _, height, slot_width = tile_values.shape
    sources = lax.axis_size("row")
    groups = lax.axis_size("col")
    per_piece = owned // height
    degree_row = degree.reshape(1, owned)
    scaled, share = pl.pallas_call(
        scale_kernel,
        out_shape=[
            jax.ShapeDtypeStruct((vectors, owned), BF16),
            jax.ShapeDtypeStruct((vectors + 16, owned), BF16),
        ],
        in_specs=[vmem(), vmem()],
        out_specs=[vmem(), vmem()],
        compiler_params=limit(2),
        name="scale",
    )(hbm(krylov_block), hbm(degree_row))
    row_bits = bits(sources)
    top = row_bits.pop()
    other = swap(scaled, top, 0)
    low = row_bits[:2]
    diag = low[0] | low[1]
    other, share = lax.optimization_barrier((other, share))
    blocks = [(0, scaled), (top, other)]
    for bit in row_bits[:1:-1]:
        stack = swap(jnp.stack([block for _, block in blocks]), bit, 0)
        blocks = blocks + [(at ^ bit, stack[place]) for place, (at, _) in enumerate(blocks)]
    base = [at for at, _ in blocks]
    named = dict(blocks)
    direct = [mask for mask in (diag, low[1], low[0])]
    relayed = [(mask, at) for at in base[1:] for mask in (diag, low[1], low[0]) if (mask ^ at) not in direct]
    pieces = [(mask, swap(scaled, mask, 0)) for mask in direct]
    early = blocks + pieces[:2]
    late = pieces[2:] + [(mask ^ at, swap(named[at], mask, 0)) for mask, at in relayed]
    other_share = swap(share, 0, bits(groups)[-1] | 1)
    order = [at for at, _ in early]
    whole = jnp.stack([block for _, block in early])
    far = [block[None] for _, block in late]
    late = [[at] for at, _ in late]
    slots = tile_column.shape[2]
    many = groups // 2
    table_shape = (sources * per_piece + 1, vectors, 2 * height)
    index, panel, table = pl.pallas_call(
        lambda *refs: load_kernel(per_piece, sources * per_piece, order, *refs),
        out_shape=[
            pltpu.SMEM((slots, block_rows), jnp.int32),
            jax.ShapeDtypeStruct((block_rows, height, slot_width), BF16),
            jax.ShapeDtypeStruct(table_shape, BF16),
        ],
        in_specs=[pl.BlockSpec(memory_space=pl.ANY)] * 3 + [vmem()],
        out_specs=[smem(), vmem(), vmem()],
        scratch_shapes=[
            pltpu.VMEM((slots, block_rows), jnp.int32),
            pltpu.VMEM((slots, block_rows), jnp.int32),
            pltpu.VMEM((slots, block_rows), jnp.int32),
            pltpu.SemaphoreType.DMA((4,)),
        ],
        compiler_params=limit(2),
        name="load",
    )(hbm(tile_column[:, 0].T), hbm(tile_live[:, 0].T), hbm(tile_values[:, 0]), whole)
    index = pltpu.with_memory_space_constraint(index, pltpu.SMEM)
    lhs = pltpu.VMEM((2, 4 * vectors, slot_width), BF16)
    table, send = pl.pallas_call(
        lambda *refs: send_kernel(groups, per_piece, late, *refs),
        out_shape=[
            jax.ShapeDtypeStruct(table_shape, BF16),
            jax.ShapeDtypeStruct((many, vectors, owned), BF16),
        ],
        in_specs=[smem()] + [vmem()] * (2 + len(far)),
        out_specs=[vmem(), vmem()],
        scratch_shapes=[lhs],
        input_output_aliases={2: 0},
        compiler_params=limit(8),
        name="send",
    )(index, panel, table, *far)
    send, other_share = lax.optimization_barrier((send, other_share))
    keep = pl.pallas_call(
        lambda *refs: keep_kernel(groups, per_piece, *refs),
        out_shape=jax.ShapeDtypeStruct((many, vectors, owned), F32),
        in_specs=[smem(), vmem(), vmem()],
        out_specs=vmem(),
        scratch_shapes=[lhs],
        compiler_params=limit(8),
        name="keep",
    )(index, panel, table)
    col_bits = bits(groups)
    last = col_bits.pop()
    for bit in col_bits:
        summed = keep + swap(send, 0, bit | 1).astype(F32)
        if bit != col_bits[-1]:
            pairs = summed.reshape((-1, 2) + summed.shape[1:])
            keep, send = pairs[:, 0], pairs[:, 1].astype(BF16)
    sums = summed.astype(BF16)
    got = swap(sums, 0, last | 1)
    pieces, gram = pl.pallas_call(
        lambda *refs: gram_kernel(last, *refs),
        out_shape=[
            jax.ShapeDtypeStruct((3 * vectors, owned), BF16),
            jax.ShapeDtypeStruct((vectors, 2 * vectors), F32),
        ],
        in_specs=[vmem()] * 4,
        out_specs=[vmem(), vmem()],
        scratch_shapes=[pltpu.VMEM((2, 4 * vectors, owned), BF16)],
        compiler_params=limit(4),
        name="gram",
    )(share, other_share, sums, got)
    for bit in col_bits:
        gram = gram + swap(gram, 0, bit | 1)
    row_bits = bits(sources)
    for bit in row_bits[2:]:
        gram = gram + swap(gram, bit, 1)
    near = [swap(gram, mask, 1) for mask in (row_bits[0] | row_bits[1], row_bits[0], row_bits[1])]
    gram = (gram + near[0]) + (near[1] + near[2])
    total_rows = sources * groups * owned
    orthonormal, quotient = pl.pallas_call(
        lambda *refs: finish_kernel(total_rows, *refs),
        out_shape=[
            jax.ShapeDtypeStruct((vectors, owned), F32),
            jax.ShapeDtypeStruct((vectors, vectors), F32),
        ],
        in_specs=[vmem(), vmem()],
        out_specs=[vmem(), vmem()],
        compiler_params=limit(4),
        name="finish",
    )(gram, pieces)
    return (orthonormal, quotient)


def solution(mesh):
    return jax.shard_map(
        on_device,
        mesh=mesh,
        in_specs=(
            P(None, ("row", "col")),
            P(("row", "col")),
            P("row", "col", None, None),
            P("row", "col", None),
            P("row", "col", None),
        ),
        out_specs=(P(None, ("row", "col")), P()),
        check_vma=False,
    )
```
